512 devices in a mesh: src: 16 (over y, core), tgt: 32 (over x, z).
Axes of the slice: x: 4, y: 8, z: 8, core: 2. Of those that a mesh axis runs over, the one named last changes fastest.
Arguments:
- noise: float32 [16384, 384], P(('src', 'tgt')), may hold values from -16 to 16
- data: float32 [32768, 384], P('tgt', 'src'), may hold values from -6 to 6
Outputs:
- velocity: float32 [16384, 384], P(('src', 'tgt'))
- target_potential: float32 [32768], P('tgt')
The draws below stay inside these ranges and needn't reach their ends.
All inputs are finite; a program needn't handle non-finite values.
Results may differ from the reference program's by a relative error of at most 0.0003.
Values sent between devices are 32-bit elements; how exact they have to be, the bound alone decides.
No kernel may reach another device: no remote copies, remote signals or barrier semaphores. Data moves between devices by JAX's collectives and lax.ppermute only.
A program may use at most 64 MiB of HBM per device.

```python
import math
import jax
import jax.numpy as jnp
from jax import lax

FEAT = 384
S_DEV = 1024
ITERS = 3
NS = 16384
NT = 32768


def draw_noise(key, part):
    base = jax.random.normal(jax.random.fold_in(key, 11), (NS, FEAT), jnp.float32)
    base = jnp.clip(base, -6.0, 6.0)
    return base


def level_of(rng, dims, pieces, smallest, high):
    gain, own = 1.0, jax.random.fold_in(rng, 6)
    for axis_at, blocks in pieces:
        draws = jnp.exp(jax.random.uniform(jax.random.fold_in(own, axis_at), (blocks,), jnp.float32, smallest / len(pieces), high / len(pieces)))
        gain = gain * jnp.repeat(draws, dims[axis_at] // blocks).reshape([-1 if axis == axis_at else 1 for axis in range(len(dims))])
    return gain


def gaussian(stream_key, extent, spread, reach, cuts=(), kind=jnp.bfloat16):
    entries = spread * jax.random.normal(stream_key, extent, jnp.float32)
    if cuts:
        entries = entries * level_of(stream_key, extent, cuts, -0.22, 0.18)
    return jnp.clip(entries, -reach, reach).astype(kind)


def setup_inputs(seed: int = 0) -> dict:
    streams_of = jax.random.split(jax.random.key(seed), 3)
    return {
        "noise": draw_noise(jax.random.fold_in(streams_of[2], 71), 0),
        "data": gaussian(streams_of[1], (NT, FEAT), 1.0, 6.0, ((0, 32), (1, 16)), jnp.float32),
    }


EPS = 0.05


def reference(noise, data):
    nblk = NS // S_DEV
    blocks = noise.reshape(nblk, S_DEV, FEAT)
    data_sq = jnp.sum(data * data, axis=1)

    def cost_of(rows):
        rows_sq = jnp.sum(rows * rows, axis=1)
        cross = jnp.dot(rows, data.T, precision=lax.Precision.HIGHEST, preferred_element_type=jnp.float32)
        return (rows_sq[:, None] + data_sq[None, :] - 2.0 * cross) / FEAT

    def row_lse(g_pot):
        def one(rows):
            z = (g_pot[None, :] - cost_of(rows)) / EPS
            top = jnp.max(z, axis=1)
            return top + jnp.log(jnp.sum(jnp.exp(z - top[:, None]), axis=1))
        return lax.map(one, blocks).reshape(NS)

    def col_lse(f_pot):
        f_blocks = f_pot.reshape(nblk, S_DEV)

        def step(carry, item):
            top, total = carry
            rows, f_part = item
            z = (f_part[:, None] - cost_of(rows)) / EPS
            local_top = jnp.max(z, axis=0)
            local_sum = jnp.sum(jnp.exp(z - local_top[None, :]), axis=0)
            new_top = jnp.maximum(top, local_top)
            total = total * jnp.exp(top - new_top) + local_sum * jnp.exp(local_top - new_top)
            return (new_top, total), None

        init = (jnp.full((NT,), -jnp.inf, dtype=jnp.float32), jnp.zeros((NT,), jnp.float32))
        (top, total), _ = lax.scan(step, init, (blocks, f_blocks))
        return top + jnp.log(total)

    g_pot = jnp.zeros((NT,), jnp.float32)
    for step_index in range(ITERS):
        f_pot = -EPS * (math.log(NS) + row_lse(g_pot))
        g_pot = -EPS * (math.log(NT) + col_lse(f_pot))

    def final(rows):
        z = (g_pot[None, :] - cost_of(rows)) / EPS
        top = jnp.max(z, axis=1)
        lrow = top + jnp.log(jnp.sum(jnp.exp(z - top[:, None]), axis=1))
        weight = jnp.exp(z - lrow[:, None])
        return jnp.dot(weight, data, precision=lax.Precision.HIGHEST, preferred_element_type=jnp.float32)

    bary = lax.map(final, blocks).reshape(NS, FEAT)
    return bary - noise, g_pot
```

```python
import math

import jax
import jax.numpy as jnp
from jax import lax
from jax.sharding import PartitionSpec as P

ITERS = 3


EPS = 0.05


def spread(value, axis):
    count = lax.axis_size(axis)
    return lax.all_to_all(jnp.broadcast_to(value[None], (count,) + value.shape), axis, 0, 0)


def total_over(local_sum, axis):
    tiles = local_sum.reshape(-1, 128)
    return jnp.sum(spread(tiles, axis), axis=0).reshape(local_sum.shape)


def lse_over(local_top, local_sum, axis):
    tiles = spread((local_top + jnp.log(local_sum)).reshape(-1, 128), axis)
    top = jnp.max(tiles, axis=0)
    merged = top + jnp.log(jnp.sum(jnp.exp(tiles - top[None]), axis=0))
    return merged.reshape(local_top.shape)


def per_device(noise, data):
    target_rows = lax.all_gather(data, "src", axis=1, tiled=True)
    own_rows, feat_width = noise.shape
    source_rows = spread(noise, "tgt").reshape(-1, feat_width)
    src_total = source_rows.shape[0] * lax.axis_size("src")
    tgt_total = target_rows.shape[0] * lax.axis_size("tgt")
    source_sq = jnp.sum(source_rows * source_rows, axis=1)
    target_sq = jnp.sum(target_rows * target_rows, axis=1)
    cross = jnp.dot(
        source_rows,
        target_rows.T,
        precision=lax.Precision.HIGHEST,
        preferred_element_type=jnp.float32,
    )
    gain = (2.0 * cross - source_sq[:, None] - target_sq[None, :]) / (feat_width * EPS)
    log_src, log_tgt = math.log(src_total), math.log(tgt_total)

    top = jnp.max(gain, axis=1)
    f_pot = -(log_src + lse_over(top, jnp.sum(jnp.exp(gain - top[:, None]), axis=1), "tgt"))
    z_tile = f_pot[:, None] + gain
    top = jnp.max(z_tile, axis=0)
    g_pot = -(log_tgt + lse_over(top, jnp.sum(jnp.exp(z_tile - top[None, :]), axis=0), "src"))
    for step_index in range(1, ITERS):
        mass = jnp.sum(jnp.exp((f_pot[:, None] + gain) + g_pot[None, :]), axis=1)
        f_pot = f_pot - (log_src + jnp.log(total_over(mass, "tgt")))
        mass = jnp.sum(jnp.exp((f_pot[:, None] + gain) + g_pot[None, :]), axis=0)
        g_pot = g_pot - (log_tgt + jnp.log(total_over(mass, "src")))
    plan = jnp.exp((f_pot[:, None] + gain) + g_pot[None, :])
    mass = jnp.sum(plan, axis=1)
    part = jnp.dot(
        plan, target_rows, precision=lax.Precision.HIGHEST, preferred_element_type=jnp.float32
    )
    count = lax.axis_size("tgt")
    part = lax.all_to_all(part.reshape(count, own_rows, feat_width), "tgt", 0, 0)
    mass = lax.all_to_all(mass.reshape(count, own_rows), "tgt", 0, 0)
    bary = jnp.sum(part, axis=0) / jnp.sum(mass, axis=0)[:, None]
    return (bary - noise, EPS * g_pot)


def solution(mesh):
    placed = (P(("src", "tgt"), None), P("tgt", "src"))
    return jax.shard_map(
        per_device,
        mesh=mesh,
        in_specs=placed,
        out_specs=(P(("src", "tgt"), None), P("tgt")),
        check_vma=False,
    )
```

```python
import math

import jax
import jax.numpy as jnp
from jax import lax
from jax.sharding import Mesh, PartitionSpec as P

ITERS = 3


EPS = 0.05
SRC = ("y", "core")


def spread(value, axis):
    count = lax.axis_size(axis)
    return lax.all_to_all(jnp.broadcast_to(value[None], (count,) + value.shape), axis, 0, 0)


def total_over(local_sum, axis):
    tiles = local_sum.reshape(-1, 128)
    return jnp.sum(spread(tiles, axis), axis=0).reshape(local_sum.shape)


def lse_over(local_top, local_sum, axis):
    tiles = spread((local_top + jnp.log(local_sum)).reshape(-1, 128), axis)
    top = jnp.max(tiles, axis=0)
    merged = top + jnp.log(jnp.sum(jnp.exp(tiles - top[None]), axis=0))
    return merged.reshape(local_top.shape)


def per_device(noise, data):
    own_rows, feat_width = noise.shape
    count = lax.axis_size("y")
    pair = lax.all_gather(data.T, "core").reshape(-1, data.shape[0])
    source_rows = spread(noise, "tgt").reshape(-1, feat_width)
    slices = [pair] + [
        lax.ppermute(pair, "y", [(i, (i + hop) % count) for i in range(count)])
        for hop in range(1, count)
    ]
    at = lax.axis_index("y")
    held = jnp.zeros((count * pair.shape[0], pair.shape[1]), jnp.float32)
    for hop, piece in enumerate(slices):
        start = (at + count - hop) % count * pair.shape[0]
        held = lax.dynamic_update_slice_in_dim(held, piece, start, 0)
    target_rows = held.T
    src_total = source_rows.shape[0] * lax.axis_size(SRC)
    tgt_total = target_rows.shape[0] * lax.axis_size("tgt")
    source_sq = jnp.sum(source_rows * source_rows, axis=1)
    target_sq = jnp.sum(target_rows * target_rows, axis=1)
    cross = jnp.dot(
        source_rows,
        target_rows.T,
        precision=lax.Precision.HIGHEST,
        preferred_element_type=jnp.float32,
    )
    gain = (2.0 * cross - source_sq[:, None] - target_sq[None, :]) / (feat_width * EPS)
    log_src, log_tgt = math.log(src_total), math.log(tgt_total)

    top = jnp.max(gain, axis=1)
    f_pot = -(log_src + lse_over(top, jnp.sum(jnp.exp(gain - top[:, None]), axis=1), "tgt"))
    z_tile = f_pot[:, None] + gain
    top = jnp.max(z_tile, axis=0)
    g_pot = -(log_tgt + lse_over(top, jnp.sum(jnp.exp(z_tile - top[None, :]), axis=0), SRC))
    for _ in range(1, ITERS):
        mass = jnp.sum(jnp.exp((f_pot[:, None] + gain) + g_pot[None, :]), axis=1)
        f_pot = f_pot - (log_src + jnp.log(total_over(mass, "tgt")))
        mass = jnp.sum(jnp.exp((f_pot[:, None] + gain) + g_pot[None, :]), axis=0)
        g_pot = g_pot - (log_tgt + jnp.log(total_over(mass, SRC)))
    plan = jnp.exp((f_pot[:, None] + gain) + g_pot[None, :])
    mass = jnp.sum(plan, axis=1)
    part = jnp.dot(
        plan, target_rows, precision=lax.Precision.HIGHEST, preferred_element_type=jnp.float32
    )
    count = lax.axis_size("tgt")
    part = lax.all_to_all(part.reshape(count, own_rows, feat_width), "tgt", 0, 0)
    mass = lax.all_to_all(mass.reshape(count, own_rows), "tgt", 0, 0)
    bary = jnp.sum(part, axis=0) / jnp.sum(mass, axis=0)[:, None]
    return (bary - noise, EPS * g_pot)


def solution(mesh):
    src, tgt = mesh.shape["src"], mesh.shape["tgt"]
    split = Mesh(mesh.devices.reshape(src // 2, 2, tgt), ("y", "core", "tgt"))
    return jax.shard_map(
        per_device,
        mesh=split,
        in_specs=(P((*SRC, "tgt"), None), P("tgt", SRC)),
        out_specs=(P((*SRC, "tgt"), None), P("tgt")),
        check_vma=False,
    )
```

```python
import functools
import math

import jax
import jax.numpy as jnp
from jax import lax
from jax.experimental import pallas as pl
from jax.experimental.pallas import tpu as pltpu
from jax.sharding import Mesh, PartitionSpec as P

ITERS = 3


EPS = 0.05
LANES = 128
BLOCK = 256
X_CHIPS = 4
INTERPRET = False
SRC, TGT = ("y", "core"), ("x", "z")
F32 = jnp.float32


def spread(value, axis):
    count = lax.axis_size(axis)
    return lax.all_to_all(jnp.broadcast_to(value[None], (count,) + value.shape), axis, 0, 0)


def diagonal():
    shape = (LANES, LANES)
    return lax.broadcasted_iota(jnp.int32, shape, 0) == lax.broadcasted_iota(jnp.int32, shape, 1)


def down(row):
    return jnp.sum(jnp.where(diagonal(), row, 0.0), axis=1, keepdims=True)


def across(column):
    return jnp.sum(jnp.where(diagonal(), column, 0.0), axis=0, keepdims=True)


def flat(tiles):
    return jnp.concatenate([tiles[t : t + 1] for t in range(tiles.shape[0])], axis=1)


def merged(ref):
    parts = ref[...]
    top = jnp.max(parts, axis=0)
    return top + jnp.log(jnp.sum(jnp.exp(parts - top[None]), axis=0))


def send(out_ref, tiles):
    out_ref[...] = jnp.broadcast_to(tiles[None], out_ref.shape)


def cost_kernel(noise_ref, data_ref, gain_ref, out_ref, rows_ref):
    data = data_ref[...]
    scale = 1.0 / (data.shape[0] * EPS)
    data_sq = jnp.sum(data * data, axis=0, keepdims=True)

    def block(b, carry):
        at = pl.ds(pl.multiple_of(b * BLOCK, BLOCK), BLOCK)
        rows = noise_ref[at, :]
        cross = jnp.dot(rows, data_ref[...], precision=lax.Precision.HIGHEST,
                        preferred_element_type=F32)
        gain = (2.0 * cross - jnp.sum(rows * rows, axis=1, keepdims=True) - data_sq) * scale
        gain_ref[at, :] = gain
        top = jnp.max(gain, axis=1, keepdims=True)
        lse = top + jnp.log(jnp.sum(jnp.exp(gain - top), axis=1, keepdims=True))
        for t in range(BLOCK // LANES):
            rows_ref[pl.ds(b * (BLOCK // LANES) + t, 1), :] = across(
                lse[t * LANES : (t + 1) * LANES])
        return carry

    lax.fori_loop(0, noise_ref.shape[0] // BLOCK, block, 0)
    send(out_ref, rows_ref[...])


def first_column_kernel(log_src, in_ref, gain_ref, f_ref, out_ref):
    f_pot = -(log_src + merged(in_ref))
    f_ref[...] = f_pot
    top = total = None
    for b in range(f_pot.shape[0]):
        z = gain_ref[b * LANES : (b + 1) * LANES, :] + down(f_pot[b : b + 1])
        here = jnp.max(z, axis=0, keepdims=True)
        if b == 0:
            top, total = here, jnp.sum(jnp.exp(z - here), axis=0, keepdims=True)
        else:
            new = jnp.maximum(top, here)
            total = total * jnp.exp(top - new) + jnp.sum(jnp.exp(z - new), axis=0, keepdims=True)
            top = new
    lse = top + jnp.log(total)
    for t in range(out_ref.shape[1]):
        out_ref[:, t : t + 1, :] = jnp.broadcast_to(
            lse[None, :, t * LANES : (t + 1) * LANES], (out_ref.shape[0], 1, LANES))


def plan_kernel(in_ref, f_ref, gain_ref, lse_ref, plan_ref, out_ref, rows_ref):
    lse = merged(in_ref)
    lse_ref[...] = lse
    column = flat(lse)
    for b in range(rows_ref.shape[0]):
        at = slice(b * LANES, (b + 1) * LANES)
        plan = jnp.exp((gain_ref[at, :] + down(f_ref[b : b + 1, :])) - column)
        plan_ref[at, :] = plan
        rows_ref[b : b + 1, :] = across(jnp.sum(plan, axis=1, keepdims=True))
    send(out_ref, rows_ref[...])


def column_kernel(src_total, in_ref, plan_ref, out_ref):
    u = 1.0 / (src_total * jnp.sum(in_ref[...], axis=0))
    total = jnp.zeros((1, plan_ref.shape[1]), F32)
    for b in range(u.shape[0]):
        total += jnp.sum(plan_ref[b * LANES : (b + 1) * LANES, :] * down(u[b : b + 1]),
                         axis=0, keepdims=True)
    for t in range(out_ref.shape[1]):
        out_ref[:, t : t + 1, :] = jnp.broadcast_to(
            total[None, :, t * LANES : (t + 1) * LANES], (out_ref.shape[0], 1, LANES))


def row_kernel(tgt_total, in_ref, plan_ref, out_ref, rows_ref):
    v = flat(1.0 / (tgt_total * jnp.sum(in_ref[...], axis=0)))
    for b in range(rows_ref.shape[0]):
        rows_ref[b : b + 1, :] = across(
            jnp.sum(plan_ref[b * LANES : (b + 1) * LANES, :] * v, axis=1, keepdims=True))
    send(out_ref, rows_ref[...])


def halves(value):
    high = value.astype(jnp.bfloat16)
    return high, (value - high.astype(F32)).astype(jnp.bfloat16)


def final_kernel(tgt_total, own_rows, in_ref, lse_ref, plan_ref, data_ref, g_ref, part_ref,
                 high_ref, low_ref):
    v = 1.0 / (tgt_total * jnp.sum(in_ref[...], axis=0))
    g_ref[...] = EPS * (jnp.log(v) - (math.log(tgt_total) + lse_ref[...]))
    v = flat(v)
    feats = data_ref.shape[0]
    scaled = data_ref[...] * v
    high_ref[:feats, :], low_ref[:feats, :] = halves(scaled)
    high_ref[feats:, :], low_ref[feats:, :] = halves(jnp.broadcast_to(v, (LANES, v.shape[1])))
    lane = lax.broadcasted_iota(jnp.int32, (8, LANES), 1)
    tiles, wide = own_rows // 8, feats // LANES

    def block(b, carry):
        high, low = halves(plan_ref[pl.ds(pl.multiple_of(b * BLOCK, BLOCK), BLOCK), :])

        def times(a, w_ref):
            return lax.dot_general(a, w_ref[...], (((1,), (1,)), ((), ())),
                                   preferred_element_type=F32)

        got = times(high, low_ref) + times(low, high_ref) + times(high, high_ref)
        for p in range(BLOCK // own_rows):
            peer = b * (BLOCK // own_rows) + p
            mass = jnp.zeros((8, LANES), F32)
            for r in range(tiles):
                at = slice(p * own_rows + r * 8, p * own_rows + r * 8 + 8)
                for c in range(wide):
                    part_ref[peer, (r * wide + c) * 8 : (r * wide + c + 1) * 8, :] = got[
                        at, c * LANES : (c + 1) * LANES]
                mass = jnp.where(lane // (LANES // tiles) == r, got[at, feats:], mass)
            part_ref[peer, tiles * wide * 8 :, :] = mass
        return carry

    lax.fori_loop(0, plan_ref.shape[0] // BLOCK, block, 0)


def last_kernel(in_ref, noise_ref, out_ref):
    rows, feats = noise_ref.shape
    tiles, wide = rows // 8, feats // LANES
    parts = jnp.sum(in_ref[...], axis=0)
    mass = parts[tiles * wide * 8 :]
    for r in range(tiles):
        inverse = 1.0 / mass[:, r * (LANES // tiles) : r * (LANES // tiles) + 1]
        for c in range(wide):
            at = (r * wide + c) * 8
            spot = (slice(r * 8, r * 8 + 8), slice(c * LANES, (c + 1) * LANES))
            out_ref[spot] = parts[at : at + 8] * inverse - noise_ref[spot]


def call(kernel, outs, *args, scratch=(), limit=24 << 20):
    return pl.pallas_call(
        kernel,
        out_shape=[jax.ShapeDtypeStruct(shape, F32) for shape in outs],
        in_specs=[pl.BlockSpec(memory_space=pltpu.VMEM)] * len(args),
        out_specs=[pl.BlockSpec(memory_space=pltpu.VMEM)] * len(outs),
        scratch_shapes=list(scratch),
        compiler_params=pltpu.CompilerParams(vmem_limit_bytes=limit),
        interpret=INTERPRET,
    )(*args)


def gathered(noise, data):
    count = lax.axis_size("y")
    at, core = lax.axis_index("y"), lax.axis_index("core")
    rows = spread(noise, TGT).reshape(-1, noise.shape[1])

    def shifted(value, hop):
        return lax.ppermute(value, "y", [(i, (i + hop) % count) for i in range(count)])

    own = data.T
    far = shifted(own, count // 2)
    both = jnp.stack([own, far])
    hops = [0] + [h for k in range(1, count // 4 + 1) for h in (k, -k)][: count // 2 - 1]
    mine = jnp.stack([both] + [shifted(both, h) for h in hops[1:]])
    theirs = lax.ppermute(mine, "core", [(0, 1), (1, 0)])
    pair = jnp.where(core == 0, jnp.stack([mine, theirs]), jnp.stack([theirs, mine]))
    pair = jnp.moveaxis(pair, 0, 2)
    feats, width = own.shape
    held = jnp.zeros((count, 2 * feats, width), F32)
    for k, hop in enumerate(hops):
        for h in range(2):
            place = (at - hop - h * (count // 2) + 2 * count) % count
            held = lax.dynamic_update_slice_in_dim(
                held, pair[k, h].reshape(1, 2 * feats, width), place, 0)
    return rows, held.reshape(-1, width)


def per_device(noise, data):
    own_rows, feats = noise.shape
    rows, columns = gathered(noise, data)
    n_rows, n_cols = rows.shape[0], columns.shape[1]
    n_src, n_tgt, n_x, n_z = (lax.axis_size(a) for a in (SRC, TGT, "x", "z"))
    src_total, tgt_total = n_rows * n_src, n_cols * n_tgt
    r_tiles, c_tiles = (n_rows // LANES, LANES), (n_cols // LANES, LANES)
    to_tgt, to_src = (n_tgt, *r_tiles), (n_src, *c_tiles)
    row_scratch = [pltpu.VMEM(r_tiles, F32)]
    square = (n_rows, n_cols)

    def swap(value, axis):
        return lax.all_to_all(value, axis, 0, 0)

    gain, message = call(cost_kernel, [square, to_tgt], rows, columns, scratch=row_scratch)
    f_pot, message = call(functools.partial(first_column_kernel, math.log(src_total)),
                          [r_tiles, to_src], swap(message, TGT), gain)
    lse, plan, message = call(plan_kernel, [c_tiles, square, to_tgt], swap(message, SRC), f_pot,
                              gain, scratch=row_scratch)
    for step_index in range(1, ITERS):
        if step_index > 1:
            (message,) = call(functools.partial(row_kernel, float(tgt_total)), [to_tgt],
                              swap(message, SRC), plan, scratch=row_scratch)
        (message,) = call(functools.partial(column_kernel, float(src_total)), [to_src],
                          swap(message, TGT), plan)
    tall = own_rows // 8 * (feats // LANES) * 8 + 8
    g_pot, part = call(
        functools.partial(final_kernel, float(tgt_total), own_rows),
        [c_tiles, (n_tgt, tall, LANES)], swap(message, SRC), lse, plan, columns,
        scratch=[pltpu.VMEM((feats + LANES, n_cols), jnp.bfloat16)] * 2)
    part = jnp.sum(swap(part.reshape(n_x, n_z * tall, LANES), "x"), axis=0)
    part = swap(part.reshape(n_z, tall, LANES), "z")
    (velocity,) = call(last_kernel, [noise.shape], part, noise)
    return velocity, g_pot.reshape(-1)


def solution(mesh):
    src, tgt = mesh.shape["src"], mesh.shape["tgt"]
    split = Mesh(mesh.devices.reshape(src // 2, 2, X_CHIPS, tgt // X_CHIPS), SRC + TGT)
    return jax.shard_map(
        per_device,
        mesh=split,
        in_specs=(P((*SRC, *TGT), None), P(TGT, SRC)),
        out_specs=(P((*SRC, *TGT), None), P(TGT)),
        check_vma=False,
    )
```

```python
import functools
import math

import jax
import jax.numpy as jnp
from jax import lax
from jax.experimental import pallas as pl
from jax.experimental.pallas import tpu as pltpu
from jax.sharding import Mesh, PartitionSpec as P

ITERS = 3


EPS = 0.05
LANES = 128
BLOCK = 256
X_CHIPS = 4
INTERPRET = False
SRC, TGT = ("yh", "yb", "core"), ("x", "zh", "zb")
ROW, COL = ("yb", "core", "x", "zb"), ("yh", "zh")
F32 = jnp.float32


def diagonal():
    shape = (LANES, LANES)
    return lax.broadcasted_iota(jnp.int32, shape, 0) == lax.broadcasted_iota(jnp.int32, shape, 1)


def down(row):
    return jnp.sum(jnp.where(diagonal(), row, 0.0), axis=1, keepdims=True)


def across(column):
    return jnp.sum(jnp.where(diagonal(), column, 0.0), axis=0, keepdims=True)


def flat(tiles):
    return jnp.concatenate([tiles[t : t + 1] for t in range(tiles.shape[0])], axis=1)


def merged(ref):
    parts = ref[...]
    top = jnp.max(parts, axis=0)
    return top + jnp.log(jnp.sum(jnp.exp(parts - top[None]), axis=0))


def send(out_ref, tiles):
    out_ref[...] = jnp.broadcast_to(tiles[None], out_ref.shape)


def cost_kernel(noise_ref, pieces_ref, gain_ref, data_ref, out_ref, rows_ref):
    pieces, deep, wide = pieces_ref.shape
    across_pieces = data_ref.shape[1] // wide
    for p in range(pieces):
        s, h = divmod(p, across_pieces)
        data_ref[s * deep : (s + 1) * deep, h * wide : (h + 1) * wide] = pieces_ref[p]
    data = data_ref[...]
    scale = 1.0 / (data.shape[0] * EPS)
    data_sq = jnp.sum(data * data, axis=0, keepdims=True)

    def block(b, carry):
        at = pl.ds(pl.multiple_of(b * BLOCK, BLOCK), BLOCK)
        rows = noise_ref[at, :]
        cross = jnp.dot(rows, data_ref[...], precision=lax.Precision.HIGHEST,
                        preferred_element_type=F32)
        gain = (2.0 * cross - jnp.sum(rows * rows, axis=1, keepdims=True) - data_sq) * scale
        gain_ref[at, :] = gain
        top = jnp.max(gain, axis=1, keepdims=True)
        lse = top + jnp.log(jnp.sum(jnp.exp(gain - top), axis=1, keepdims=True))
        for t in range(BLOCK // LANES):
            rows_ref[pl.ds(b * (BLOCK // LANES) + t, 1), :] = across(
                lse[t * LANES : (t + 1) * LANES])
        return carry

    lax.fori_loop(0, noise_ref.shape[0] // BLOCK, block, 0)
    send(out_ref, rows_ref[...])


def first_column_kernel(log_src, in_ref, gain_ref, f_ref, out_ref):
    f_pot = -(log_src + merged(in_ref))
    f_ref[...] = f_pot
    top = total = None
    for b in range(f_pot.shape[0]):
        z = gain_ref[b * LANES : (b + 1) * LANES, :] + down(f_pot[b : b + 1])
        here = jnp.max(z, axis=0, keepdims=True)
        if b == 0:
            top, total = here, jnp.sum(jnp.exp(z - here), axis=0, keepdims=True)
        else:
            new = jnp.maximum(top, here)
            total = total * jnp.exp(top - new) + jnp.sum(jnp.exp(z - new), axis=0, keepdims=True)
            top = new
    lse = top + jnp.log(total)
    for t in range(out_ref.shape[1]):
        out_ref[:, t : t + 1, :] = jnp.broadcast_to(
            lse[None, :, t * LANES : (t + 1) * LANES], (out_ref.shape[0], 1, LANES))


def plan_kernel(in_ref, f_ref, gain_ref, lse_ref, plan_ref, out_ref, rows_ref):
    lse = merged(in_ref)
    lse_ref[...] = lse
    column = flat(lse)
    for b in range(rows_ref.shape[0]):
        at = slice(b * LANES, (b + 1) * LANES)
        plan = jnp.exp((gain_ref[at, :] + down(f_ref[b : b + 1, :])) - column)
        plan_ref[at, :] = plan
        rows_ref[b : b + 1, :] = across(jnp.sum(plan, axis=1, keepdims=True))
    send(out_ref, rows_ref[...])


def column_kernel(src_total, in_ref, plan_ref, out_ref):
    u = 1.0 / (src_total * jnp.sum(in_ref[...], axis=0))
    total = jnp.zeros((1, plan_ref.shape[1]), F32)
    for b in range(u.shape[0]):
        total += jnp.sum(plan_ref[b * LANES : (b + 1) * LANES, :] * down(u[b : b + 1]),
                         axis=0, keepdims=True)
    for t in range(out_ref.shape[1]):
        out_ref[:, t : t + 1, :] = jnp.broadcast_to(
            total[None, :, t * LANES : (t + 1) * LANES], (out_ref.shape[0], 1, LANES))


def row_kernel(tgt_total, in_ref, plan_ref, out_ref, rows_ref):
    v = flat(1.0 / (tgt_total * jnp.sum(in_ref[...], axis=0)))
    for b in range(rows_ref.shape[0]):
        rows_ref[b : b + 1, :] = across(
            jnp.sum(plan_ref[b * LANES : (b + 1) * LANES, :] * v, axis=1, keepdims=True))
    send(out_ref, rows_ref[...])


def halves(value):
    high = value.astype(jnp.bfloat16)
    return high, (value - high.astype(F32)).astype(jnp.bfloat16)


def final_kernel(tgt_total, own_rows, in_ref, lse_ref, plan_ref, data_ref, g_ref, part_ref,
                 high_ref, low_ref):
    v = 1.0 / (tgt_total * jnp.sum(in_ref[...], axis=0))
    g_ref[...] = EPS * (jnp.log(v) - (math.log(tgt_total) + lse_ref[...]))
    v = flat(v)
    feats = data_ref.shape[0]
    scaled = data_ref[...] * v
    high_ref[:feats, :], low_ref[:feats, :] = halves(scaled)
    high_ref[feats:, :], low_ref[feats:, :] = halves(jnp.broadcast_to(v, (LANES, v.shape[1])))
    lane = lax.broadcasted_iota(jnp.int32, (8, LANES), 1)
    tiles, wide = own_rows // 8, feats // LANES

    def block(b, carry):
        high, low = halves(plan_ref[pl.ds(pl.multiple_of(b * BLOCK, BLOCK), BLOCK), :])

        def times(a, w_ref):
            return lax.dot_general(a, w_ref[...], (((1,), (1,)), ((), ())),
                                   preferred_element_type=F32)

        got = times(high, low_ref) + times(low, high_ref) + times(high, high_ref)
        for p in range(BLOCK // own_rows):
            peer = b * (BLOCK // own_rows) + p
            mass = jnp.zeros((8, LANES), F32)
            for r in range(tiles):
                at = slice(p * own_rows + r * 8, p * own_rows + r * 8 + 8)
                for c in range(wide):
                    part_ref[peer, (r * wide + c) * 8 : (r * wide + c + 1) * 8, :] = got[
                        at, c * LANES : (c + 1) * LANES]
                mass = jnp.where(lane // (LANES // tiles) == r, got[at, feats:], mass)
            part_ref[peer, tiles * wide * 8 :, :] = mass
        return carry

    lax.fori_loop(0, plan_ref.shape[0] // BLOCK, block, 0)


def last_kernel(in_ref, noise_ref, out_ref):
    rows, feats = noise_ref.shape
    tiles, wide = rows // 8, feats // LANES
    parts = jnp.sum(in_ref[...], axis=0)
    mass = parts[tiles * wide * 8 :]
    for r in range(tiles):
        inverse = 1.0 / mass[:, r * (LANES // tiles) : r * (LANES // tiles) + 1]
        for c in range(wide):
            at = (r * wide + c) * 8
            spot = (slice(r * 8, r * 8 + 8), slice(c * LANES, (c + 1) * LANES))
            out_ref[spot] = parts[at : at + 8] * inverse - noise_ref[spot]


def call(kernel, outs, *args, scratch=(), limit=24 << 20):
    return pl.pallas_call(
        kernel,
        out_shape=[jax.ShapeDtypeStruct(shape, F32) for shape in outs],
        in_specs=[pl.BlockSpec(memory_space=pltpu.VMEM)] * len(args),
        out_specs=[pl.BlockSpec(memory_space=pltpu.VMEM)] * len(outs),
        scratch_shapes=list(scratch),
        compiler_params=pltpu.CompilerParams(vmem_limit_bytes=limit),
        interpret=INTERPRET,
    )(*args)


def swap(value, axis):
    return lax.all_to_all(value, axis, 0, 0)


def joined(value, axis, spot):
    other = lax.ppermute(value, axis, [(0, 1), (1, 0)])
    first = lax.axis_index(axis) == 0
    return jnp.stack([jnp.where(first, value, other), jnp.where(first, other, value)], spot)


def gathered(noise, data):
    n_yh, n_zh, n_x = lax.axis_size("yh"), lax.axis_size("zh"), lax.axis_size("x")
    at = lax.axis_index("x")
    quarters = jnp.swapaxes(data.T.reshape(data.shape[1], 4, -1), 0, 1)
    shape = (n_yh, 4, n_zh, *quarters.shape[1:])
    pieces = jnp.broadcast_to(quarters[None, :, None], shape)
    pieces = swap(pieces.reshape(-1, *shape[3:]), ("yh", "yb", "core", "zh"))
    hops = [h for k in range(1, n_x // 2 + 1) for h in (k, -k)][: n_x - 1]
    rows = jnp.zeros((n_x, *noise.shape), F32)
    rows = lax.dynamic_update_slice_in_dim(rows, noise[None], at, 0)
    for hop in hops:
        piece = lax.ppermute(noise, "x", [(i, (i + hop) % n_x) for i in range(n_x)])
        rows = lax.dynamic_update_slice_in_dim(
            rows, piece[None], (at - hop + n_x) % n_x, 0)
    rows = joined(joined(joined(rows, "yb", 0), "zb", 2), "core", 1)
    return rows.reshape(-1, noise.shape[1]), pieces


def per_device(noise, data):
    own_rows, feats = noise.shape
    rows, pieces = gathered(noise, data)
    n_row, n_col = lax.axis_size(ROW), lax.axis_size(COL)
    n_rows, n_cols = rows.shape[0], pieces.shape[2] * lax.axis_size("zh")
    src_total, tgt_total = n_rows * n_col, n_cols * n_row
    r_tiles, c_tiles = (n_rows // LANES, LANES), (n_cols // LANES, LANES)
    to_row, to_col = (n_row, *r_tiles), (n_col, *c_tiles)
    row_scratch = [pltpu.VMEM(r_tiles, F32)]
    square = (n_rows, n_cols)

    gain, columns, message = call(cost_kernel, [square, (feats, n_cols), to_row], rows, pieces,
                                  scratch=row_scratch)
    f_pot, message = call(functools.partial(first_column_kernel, math.log(src_total)),
                          [r_tiles, to_col], swap(message, ROW), gain)
    lse, plan, message = call(plan_kernel, [c_tiles, square, to_row], swap(message, COL), f_pot,
                              gain, scratch=row_scratch)
    for step_index in range(1, ITERS):
        if step_index > 1:
            (message,) = call(functools.partial(row_kernel, float(tgt_total)), [to_row],
                              swap(message, COL), plan, scratch=row_scratch)
        (message,) = call(functools.partial(column_kernel, float(src_total)), [to_col],
                          swap(message, ROW), plan)
    tall = own_rows // 8 * (feats // LANES) * 8 + 8
    g_pot, part = call(
        functools.partial(final_kernel, float(tgt_total), own_rows),
        [c_tiles, (n_row, tall, LANES)], swap(message, COL), lse, plan, columns,
        scratch=[pltpu.VMEM((feats + LANES, n_cols), jnp.bfloat16)] * 2)
    part = swap(part, ROW)
    own = lax.dynamic_index_in_dim(
        g_pot.reshape(lax.axis_size("zh"), -1), lax.axis_index("zh"), 0, False)
    potential = joined(joined(own, "core", 0), "yb", 0).reshape(-1)
    (velocity,) = call(last_kernel, [noise.shape], part, noise)
    return velocity, potential


def solution(mesh):
    src, tgt = mesh.shape["src"], mesh.shape["tgt"]
    split = Mesh(
        mesh.devices.reshape(src // 4, 2, 2, X_CHIPS, tgt // X_CHIPS // 2, 2), SRC + TGT)
    return jax.shard_map(
        per_device,
        mesh=split,
        in_specs=(P((*SRC, *TGT), None), P(TGT, SRC)),
        out_specs=(P((*SRC, *TGT), None), P(TGT)),
        check_vma=False,
    )
```

```python
import functools
import math

import jax
import jax.numpy as jnp
from jax import lax
from jax.experimental import pallas as pl
from jax.experimental.pallas import tpu as pltpu
from jax.sharding import Mesh, PartitionSpec as P

ITERS = 3


EPS = 0.05
LANES = 128
BLOCK = 256
X_CHIPS = 4
INTERPRET = False
SRC, TGT = ("y", "core"), ("x", "z")
F32 = jnp.float32


def spread(value, axis):
    count = lax.axis_size(axis)
    return lax.all_to_all(jnp.broadcast_to(value[None], (count,) + value.shape), axis, 0, 0)


def diagonal():
    shape = (LANES, LANES)
    return lax.broadcasted_iota(jnp.int32, shape, 0) == lax.broadcasted_iota(jnp.int32, shape, 1)


def down(row):
    return jnp.sum(jnp.where(diagonal(), row, 0.0), axis=1, keepdims=True)


def across(column):
    return jnp.sum(jnp.where(diagonal(), column, 0.0), axis=0, keepdims=True)


def flat(tiles):
    return jnp.concatenate([tiles[t : t + 1] for t in range(tiles.shape[0])], axis=1)


def merged(ref):
    parts = ref[...]
    top = jnp.max(parts, axis=0)
    return top + jnp.log(jnp.sum(jnp.exp(parts - top[None]), axis=0))


def send(out_ref, tiles):
    out_ref[...] = jnp.broadcast_to(tiles[None], out_ref.shape)


def thirds(value):
    high = value.astype(jnp.bfloat16)
    rest = value - high.astype(F32)
    middle = rest.astype(jnp.bfloat16)
    return high, middle, (rest - middle.astype(F32)).astype(jnp.bfloat16)


LEFT, RIGHT = (2, 0, 1, 1, 0, 0), (0, 2, 1, 0, 1, 0)


def pile_kernel(*refs):
    for k, ref in enumerate(refs[:-1]):
        refs[-1][k] = ref[...]


def cost_kernel(spot_ref, mine_ref, theirs_ref, noise_ref, gain_ref, data_ref, out_ref,
                rows_ref, terms_ref):
    groups, halfs, deep, _ = mine_ref.shape
    for c, ref in enumerate((mine_ref, theirs_ref)):
        for k in range(groups):
            for h in range(halfs):
                spot = pl.multiple_of(spot_ref[(c * groups + k) * halfs + h], 8)
                data_ref[pl.ds(spot, deep), :] = ref[k, h]
    data = data_ref[...]
    feats = data.shape[0]
    scale = 1.0 / (feats * EPS)
    data_sq = jnp.sum(data * data, axis=0, keepdims=True)
    parts = thirds(data)
    for k, which in enumerate(RIGHT):
        terms_ref[k * feats : (k + 1) * feats, :] = parts[which]
    for b in range(noise_ref.shape[0] // BLOCK):
        at = slice(b * BLOCK, (b + 1) * BLOCK)
        rows = noise_ref[at, :]
        parts = thirds(rows)
        cross = jnp.dot(jnp.concatenate([parts[which] for which in LEFT], axis=1),
                        terms_ref[...], preferred_element_type=F32)
        gain = (2.0 * cross - jnp.sum(rows * rows, axis=1, keepdims=True) - data_sq) * scale
        gain_ref[at, :] = gain
        top = jnp.max(gain, axis=1, keepdims=True)
        lse = top + jnp.log(jnp.sum(jnp.exp(gain - top), axis=1, keepdims=True))
        for t in range(BLOCK // LANES):
            spot = b * (BLOCK // LANES) + t
            rows_ref[spot : spot + 1, :] = across(lse[t * LANES : (t + 1) * LANES])
    send(out_ref, rows_ref[...])


def first_column_kernel(log_src, in_ref, gain_ref, f_ref, out_ref):
    f_pot = -(log_src + merged(in_ref))
    f_ref[...] = f_pot
    top = total = None
    for b in range(f_pot.shape[0]):
        z = gain_ref[b * LANES : (b + 1) * LANES, :] + down(f_pot[b : b + 1])
        here = jnp.max(z, axis=0, keepdims=True)
        if b == 0:
            top, total = here, jnp.sum(jnp.exp(z - here), axis=0, keepdims=True)
        else:
            new = jnp.maximum(top, here)
            total = total * jnp.exp(top - new) + jnp.sum(jnp.exp(z - new), axis=0, keepdims=True)
            top = new
    lse = top + jnp.log(total)
    for t in range(out_ref.shape[1]):
        out_ref[:, t : t + 1, :] = jnp.broadcast_to(
            lse[None, :, t * LANES : (t + 1) * LANES], (out_ref.shape[0], 1, LANES))


def plan_kernel(in_ref, f_ref, gain_ref, lse_ref, plan_ref, out_ref, rows_ref):
    lse = merged(in_ref)
    lse_ref[...] = lse
    column = flat(lse)
    for b in range(rows_ref.shape[0]):
        at = slice(b * LANES, (b + 1) * LANES)
        plan = jnp.exp((gain_ref[at, :] + down(f_ref[b : b + 1, :])) - column)
        plan_ref[at, :] = plan
        rows_ref[b : b + 1, :] = across(jnp.sum(plan, axis=1, keepdims=True))
    send(out_ref, rows_ref[...])


def column_kernel(src_total, in_ref, plan_ref, out_ref):
    u = 1.0 / (src_total * jnp.sum(in_ref[...], axis=0))
    total = jnp.zeros((1, plan_ref.shape[1]), F32)
    for b in range(u.shape[0]):
        total += jnp.sum(plan_ref[b * LANES : (b + 1) * LANES, :] * down(u[b : b + 1]),
                         axis=0, keepdims=True)
    for t in range(out_ref.shape[1]):
        out_ref[:, t : t + 1, :] = jnp.broadcast_to(
            total[None, :, t * LANES : (t + 1) * LANES], (out_ref.shape[0], 1, LANES))


def row_kernel(tgt_total, in_ref, plan_ref, out_ref, rows_ref):
    v = flat(1.0 / (tgt_total * jnp.sum(in_ref[...], axis=0)))
    for b in range(rows_ref.shape[0]):
        rows_ref[b : b + 1, :] = across(
            jnp.sum(plan_ref[b * LANES : (b + 1) * LANES, :] * v, axis=1, keepdims=True))
    send(out_ref, rows_ref[...])


def halves(value):
    high = value.astype(jnp.bfloat16)
    return high, (value - high.astype(F32)).astype(jnp.bfloat16)


def final_kernel(tgt_total, own_rows, in_ref, lse_ref, plan_ref, data_ref, g_ref, part_ref,
                 high_ref, low_ref):
    v = 1.0 / (tgt_total * jnp.sum(in_ref[...], axis=0))
    g_ref[...] = EPS * (jnp.log(v) - (math.log(tgt_total) + lse_ref[...]))
    v = flat(v)
    feats = data_ref.shape[0]
    scaled = data_ref[...] * v
    high_ref[:feats, :], low_ref[:feats, :] = halves(scaled)
    high_ref[feats:, :], low_ref[feats:, :] = halves(jnp.broadcast_to(v, (LANES, v.shape[1])))
    lane = lax.broadcasted_iota(jnp.int32, (8, LANES), 1)
    tiles, wide = own_rows // 8, feats // LANES

    def block(b, carry):
        high, low = halves(plan_ref[pl.ds(pl.multiple_of(b * BLOCK, BLOCK), BLOCK), :])

        def times(a, w_ref):
            return lax.dot_general(a, w_ref[...], (((1,), (1,)), ((), ())),
                                   preferred_element_type=F32)

        got = times(high, low_ref) + times(low, high_ref) + times(high, high_ref)
        for p in range(BLOCK // own_rows):
            peer = b * (BLOCK // own_rows) + p
            mass = jnp.zeros((8, LANES), F32)
            for r in range(tiles):
                at = slice(p * own_rows + r * 8, p * own_rows + r * 8 + 8)
                for c in range(wide):
                    part_ref[peer, (r * wide + c) * 8 : (r * wide + c + 1) * 8, :] = got[
                        at, c * LANES : (c + 1) * LANES]
                mass = jnp.where(lane // (LANES // tiles) == r, got[at, feats:], mass)
            part_ref[peer, tiles * wide * 8 :, :] = mass
        return carry

    lax.fori_loop(0, plan_ref.shape[0] // BLOCK, block, 0)


def last_kernel(in_ref, noise_ref, out_ref):
    rows, feats = noise_ref.shape
    tiles, wide = rows // 8, feats // LANES
    parts = jnp.sum(in_ref[...], axis=0)
    mass = parts[tiles * wide * 8 :]
    for r in range(tiles):
        inverse = 1.0 / mass[:, r * (LANES // tiles) : r * (LANES // tiles) + 1]
        for c in range(wide):
            at = (r * wide + c) * 8
            spot = (slice(r * 8, r * 8 + 8), slice(c * LANES, (c + 1) * LANES))
            out_ref[spot] = parts[at : at + 8] * inverse - noise_ref[spot]


def call(kernel, outs, *args, scratch=(), limit=24 << 20):
    return pl.pallas_call(
        kernel,
        out_shape=[jax.ShapeDtypeStruct(shape, F32) for shape in outs],
        in_specs=[pl.BlockSpec(memory_space=pltpu.VMEM if a.dtype == F32 else pltpu.SMEM)
                  for a in args],
        out_specs=[pl.BlockSpec(memory_space=pltpu.VMEM)] * len(outs),
        scratch_shapes=list(scratch),
        compiler_params=pltpu.CompilerParams(vmem_limit_bytes=limit),
        interpret=INTERPRET,
    )(*args)


def gathered(noise, data):
    count = lax.axis_size("y")
    at, core = lax.axis_index("y"), lax.axis_index("core")

    def shifted(value, hop):
        return lax.ppermute(value, "y", [(i, (i + hop) % count) for i in range(count)])

    hops = [0] + [h for k in range(1, count // 4 + 1) for h in (k, -k)][: count // 2 - 1]
    own = data.T
    far = shifted(own, count // 2)
    rows = spread(noise, "z").reshape(-1, noise.shape[1])
    both = jnp.stack([own, far])
    near = [shifted(both, h) for h in hops[1:]]
    rows = spread(rows, "x").reshape(-1, noise.shape[1])
    (mine,) = call(pile_kernel, [(count // 2, *both.shape)], both, *near, limit=8 << 20)
    theirs = lax.ppermute(mine, "core", [(0, 1), (1, 0)])
    spots = [2 * ((at - hop - h * (count // 2) + 2 * count) % count) for hop in hops
             for h in range(2)]
    spots = jnp.stack([s + c for c in (core, 1 - core) for s in spots])
    return rows, mine, theirs, (spots * own.shape[0]).astype(jnp.int32)


def per_device(noise, data):
    own_rows, feats = noise.shape
    rows, mine, theirs, spots = gathered(noise, data)
    n_rows, n_cols = rows.shape[0], mine.shape[-1]
    n_src, n_tgt, n_x, n_z = (lax.axis_size(a) for a in (SRC, TGT, "x", "z"))
    src_total, tgt_total = n_rows * n_src, n_cols * n_tgt
    r_tiles, c_tiles = (n_rows // LANES, LANES), (n_cols // LANES, LANES)
    to_tgt, to_src = (n_tgt, *r_tiles), (n_src, *c_tiles)
    row_scratch = [pltpu.VMEM(r_tiles, F32)]
    square = (n_rows, n_cols)

    def swap(value, axis):
        return lax.all_to_all(value, axis, 0, 0)

    gain, columns, message = call(
        cost_kernel, [square, (feats, n_cols), to_tgt], spots, mine, theirs, rows,
        scratch=row_scratch + [pltpu.VMEM((len(LEFT) * feats, n_cols), jnp.bfloat16)])
    f_pot, message = call(functools.partial(first_column_kernel, math.log(src_total)),
                          [r_tiles, to_src], swap(message, TGT), gain)
    lse, plan, message = call(plan_kernel, [c_tiles, square, to_tgt], swap(message, SRC), f_pot,
                              gain, scratch=row_scratch)
    for step_index in range(1, ITERS):
        if step_index > 1:
            (message,) = call(functools.partial(row_kernel, float(tgt_total)), [to_tgt],
                              swap(message, SRC), plan, scratch=row_scratch)
        (message,) = call(functools.partial(column_kernel, float(src_total)), [to_src],
                          swap(message, TGT), plan)
    tall = own_rows // 8 * (feats // LANES) * 8 + 8
    g_pot, part = call(
        functools.partial(final_kernel, float(tgt_total), own_rows),
        [c_tiles, (n_tgt, tall, LANES)], swap(message, SRC), lse, plan, columns,
        scratch=[pltpu.VMEM((feats + LANES, n_cols), jnp.bfloat16)] * 2)
    part = jnp.sum(swap(part.reshape(n_x, n_z * tall, LANES), "x"), axis=0)
    part = swap(part.reshape(n_z, tall, LANES), "z")
    (velocity,) = call(last_kernel, [noise.shape], part, noise)
    return velocity, g_pot.reshape(-1)


def solution(mesh):
    src, tgt = mesh.shape["src"], mesh.shape["tgt"]
    split = Mesh(mesh.devices.reshape(src // 2, 2, X_CHIPS, tgt // X_CHIPS), SRC + TGT)
    return jax.shard_map(
        per_device,
        mesh=split,
        in_specs=(P((*SRC, *TGT), None), P(TGT, SRC)),
        out_specs=(P((*SRC, *TGT), None), P(TGT)),
        check_vma=False,
    )
```

```python
import functools
import math

import jax
import jax.numpy as jnp
from jax import lax
from jax.experimental import pallas as pl
from jax.experimental.pallas import tpu as pltpu
from jax.sharding import Mesh, PartitionSpec as P

ITERS = 3


EPS = 0.05
LANES = 128
BLOCK = 256
X_CHIPS = 4
INTERPRET = False
LIMIT = 24 << 20
SRC, TGT, NEAR, FAR = ("y", "core"), ("x", "zh", "zb"), ("x", "zb"), "zh"
F32 = jnp.float32


def spread(value, axis):
    count = lax.axis_size(axis)
    return lax.all_to_all(jnp.broadcast_to(value[None], (count,) + value.shape), axis, 0, 0)


def diagonal():
    shape = (LANES, LANES)
    return lax.broadcasted_iota(jnp.int32, shape, 0) == lax.broadcasted_iota(jnp.int32, shape, 1)


def down(row):
    return jnp.sum(jnp.where(diagonal(), row, 0.0), axis=1, keepdims=True)


def across(column):
    return jnp.sum(jnp.where(diagonal(), column, 0.0), axis=0, keepdims=True)


def flat(tiles):
    return jnp.concatenate([tiles[t : t + 1] for t in range(tiles.shape[0])], axis=1)


def merged(ref):
    parts = ref[...]
    top = jnp.max(parts, axis=0)
    return top + jnp.log(jnp.sum(jnp.exp(parts - top[None]), axis=0))


def send(out_ref, tiles):
    out_ref[...] = jnp.broadcast_to(tiles[None], out_ref.shape)


def thirds(value):
    high = value.astype(jnp.bfloat16)
    rest = value - high.astype(F32)
    middle = rest.astype(jnp.bfloat16)
    return high, middle, (rest - middle.astype(F32)).astype(jnp.bfloat16)


LEFT, RIGHT = (2, 0, 1, 1, 0, 0), (0, 2, 1, 0, 1, 0)


def pile_kernel(*refs):
    for k, ref in enumerate(refs[:-1]):
        refs[-1][k] = ref[...]


def order_kernel(hops, count, mine_ref, theirs_ref, data_ref):
    at, core = lax.axis_index("y"), lax.axis_index("core")
    groups, halfs, deep, _ = mine_ref.shape
    for c, ref in enumerate((mine_ref, theirs_ref)):
        for k in range(groups):
            for h in range(halfs):
                chip = lax.rem(at + (2 * count - hops[k] - h * (count // 2)), count)
                spot = (2 * chip + (1 - core if c else core)) * deep
                data_ref[pl.ds(pl.multiple_of(spot, 8), deep), :] = ref[k, h]


def cost_kernel(data_ref, noise_ref, gain_ref, out_ref, rows_ref, terms_ref):
    data = data_ref[...]
    feats = data.shape[0]
    scale = 1.0 / (feats * EPS)
    data_sq = jnp.sum(data * data, axis=0, keepdims=True)
    parts = thirds(data)
    for k, which in enumerate(RIGHT):
        terms_ref[k * feats : (k + 1) * feats, :] = parts[which]
    for b in range(noise_ref.shape[0] // BLOCK):
        at = slice(b * BLOCK, (b + 1) * BLOCK)
        rows = noise_ref[at, :]
        parts = thirds(rows)
        cross = jnp.dot(jnp.concatenate([parts[which] for which in LEFT], axis=1),
                        terms_ref[...], preferred_element_type=F32)
        gain = (2.0 * cross - jnp.sum(rows * rows, axis=1, keepdims=True) - data_sq) * scale
        gain_ref[at, :] = gain
        top = jnp.max(gain, axis=1, keepdims=True)
        lse = top + jnp.log(jnp.sum(jnp.exp(gain - top), axis=1, keepdims=True))
        for t in range(BLOCK // LANES):
            spot = b * (BLOCK // LANES) + t
            rows_ref[spot : spot + 1, :] = across(lse[t * LANES : (t + 1) * LANES])
    send(out_ref, rows_ref[...])


def first_column_kernel(log_src, in_ref, gain_ref, f_ref, out_ref):
    f_pot = -(log_src + merged(in_ref))
    f_ref[...] = f_pot
    top = total = None
    for b in range(f_pot.shape[0]):
        z = gain_ref[b * LANES : (b + 1) * LANES, :] + down(f_pot[b : b + 1])
        here = jnp.max(z, axis=0, keepdims=True)
        if b == 0:
            top, total = here, jnp.sum(jnp.exp(z - here), axis=0, keepdims=True)
        else:
            new = jnp.maximum(top, here)
            total = total * jnp.exp(top - new) + jnp.sum(jnp.exp(z - new), axis=0, keepdims=True)
            top = new
    lse = top + jnp.log(total)
    for t in range(out_ref.shape[1]):
        out_ref[:, t : t + 1, :] = jnp.broadcast_to(
            lse[None, :, t * LANES : (t + 1) * LANES], (out_ref.shape[0], 1, LANES))


def plan_kernel(in_ref, f_ref, gain_ref, lse_ref, plan_ref, out_ref, rows_ref):
    lse = merged(in_ref)
    lse_ref[...] = lse
    column = flat(lse)
    for b in range(rows_ref.shape[0]):
        at = slice(b * LANES, (b + 1) * LANES)
        plan = jnp.exp((gain_ref[at, :] + down(f_ref[b : b + 1, :])) - column)
        plan_ref[at, :] = plan
        rows_ref[b : b + 1, :] = across(jnp.sum(plan, axis=1, keepdims=True))
    send(out_ref, rows_ref[...])


def column_kernel(src_total, in_ref, plan_ref, out_ref):
    u = 1.0 / (src_total * jnp.sum(in_ref[...], axis=0))
    total = jnp.zeros((1, plan_ref.shape[1]), F32)
    for b in range(u.shape[0]):
        total += jnp.sum(plan_ref[b * LANES : (b + 1) * LANES, :] * down(u[b : b + 1]),
                         axis=0, keepdims=True)
    for t in range(out_ref.shape[1]):
        out_ref[:, t : t + 1, :] = jnp.broadcast_to(
            total[None, :, t * LANES : (t + 1) * LANES], (out_ref.shape[0], 1, LANES))


def row_kernel(tgt_total, in_ref, plan_ref, out_ref, rows_ref):
    v = flat(1.0 / (tgt_total * jnp.sum(in_ref[...], axis=0)))
    for b in range(rows_ref.shape[0]):
        rows_ref[b : b + 1, :] = across(
            jnp.sum(plan_ref[b * LANES : (b + 1) * LANES, :] * v, axis=1, keepdims=True))
    send(out_ref, rows_ref[...])


def halves(value):
    high = value.astype(jnp.bfloat16)
    return high, (value - high.astype(F32)).astype(jnp.bfloat16)


def final_kernel(tgt_total, own_rows, in_ref, lse_ref, plan_ref, data_ref, g_ref, part_ref,
                 high_ref, low_ref):
    v = 1.0 / (tgt_total * jnp.sum(in_ref[...], axis=0))
    g_ref[...] = EPS * (jnp.log(v) - (math.log(tgt_total) + lse_ref[...]))
    v = flat(v)
    feats = data_ref.shape[0]
    scaled = data_ref[...] * v
    high_ref[:feats, :], low_ref[:feats, :] = halves(scaled)
    high_ref[feats:, :], low_ref[feats:, :] = halves(jnp.broadcast_to(v, (LANES, v.shape[1])))
    lane = lax.broadcasted_iota(jnp.int32, (8, LANES), 1)
    tiles, wide = own_rows // 8, feats // LANES

    def block(b, carry):
        high, low = halves(plan_ref[pl.ds(pl.multiple_of(b * BLOCK, BLOCK), BLOCK), :])

        def times(a, w_ref):
            return lax.dot_general(a, w_ref[...], (((1,), (1,)), ((), ())),
                                   preferred_element_type=F32)

        got = times(high, low_ref) + times(low, high_ref) + times(high, high_ref)
        for p in range(BLOCK // own_rows):
            peer = b * (BLOCK // own_rows) + p
            mass = jnp.zeros((8, LANES), F32)
            for r in range(tiles):
                at = slice(p * own_rows + r * 8, p * own_rows + r * 8 + 8)
                for c in range(wide):
                    part_ref[peer, (r * wide + c) * 8 : (r * wide + c + 1) * 8, :] = got[
                        at, c * LANES : (c + 1) * LANES]
                mass = jnp.where(lane // (LANES // tiles) == r, got[at, feats:], mass)
            part_ref[peer, tiles * wide * 8 :, :] = mass
        return carry

    lax.fori_loop(0, plan_ref.shape[0] // BLOCK, block, 0)


def last_kernel(in_ref, noise_ref, out_ref):
    rows, feats = noise_ref.shape
    tiles, wide = rows // 8, feats // LANES
    parts = jnp.sum(in_ref[...], axis=0)
    mass = parts[tiles * wide * 8 :]
    for r in range(tiles):
        inverse = 1.0 / mass[:, r * (LANES // tiles) : r * (LANES // tiles) + 1]
        for c in range(wide):
            at = (r * wide + c) * 8
            spot = (slice(r * 8, r * 8 + 8), slice(c * LANES, (c + 1) * LANES))
            out_ref[spot] = parts[at : at + 8] * inverse - noise_ref[spot]


def call(kernel, outs, *args, scratch=(), limit=LIMIT):
    return pl.pallas_call(
        kernel,
        out_shape=[jax.ShapeDtypeStruct(o, F32) if isinstance(o, tuple) else o for o in outs],
        in_specs=[pl.BlockSpec(memory_space=pltpu.VMEM)] * len(args),
        out_specs=[pl.BlockSpec(memory_space=pltpu.VMEM)] * len(outs),
        scratch_shapes=list(scratch),
        compiler_params=pltpu.CompilerParams(vmem_limit_bytes=limit),
        interpret=INTERPRET,
    )(*args)


def gathered(noise, data):
    count = lax.axis_size("y")

    def shifted(value, hop):
        return lax.ppermute(value, "y", [(i, (i + hop) % count) for i in range(count)])

    hops = [0] + [h for k in range(1, count // 4 + 1) for h in (k, -k)][: count // 2 - 1]
    own = data.T
    rows = spread(noise, FAR).reshape(-1, noise.shape[1])
    far = shifted(own, count // 2)
    both = jnp.stack([own, far])
    near = [shifted(both, h) for h in hops[1:]]
    rows = spread(rows, NEAR).reshape(-1, noise.shape[1])
    (mine,) = call(pile_kernel, [(count // 2, *both.shape)], both, *near, limit=8 << 20)
    theirs = lax.ppermute(mine, "core", [(0, 1), (1, 0)])
    (columns,) = call(functools.partial(order_kernel, hops, count),
                      [(2 * count * own.shape[0], own.shape[1])], mine, theirs,
                      limit=8 << 20)
    return rows, columns


def per_device(noise, data):
    own_rows, feats = noise.shape
    rows, columns = gathered(noise, data)
    n_rows, n_cols = rows.shape[0], columns.shape[1]
    n_src, n_tgt, n_near, n_far = (lax.axis_size(a) for a in (SRC, TGT, NEAR, FAR))
    src_total, tgt_total = n_rows * n_src, n_cols * n_tgt
    r_tiles, c_tiles = (n_rows // LANES, LANES), (n_cols // LANES, LANES)
    to_tgt, to_src = (n_tgt, *r_tiles), (n_src, *c_tiles)
    row_scratch = [pltpu.VMEM(r_tiles, F32)]
    square = (n_rows, n_cols)

    def swap(value, axis):
        return lax.all_to_all(value, axis, 0, 0)

    gain, message = call(
        cost_kernel, [square, to_tgt], columns, rows,
        scratch=row_scratch + [pltpu.VMEM((len(LEFT) * feats, n_cols), jnp.bfloat16)])
    f_pot, message = call(functools.partial(first_column_kernel, math.log(src_total)),
                          [r_tiles, to_src], swap(message, TGT), gain)
    lse, plan, message = call(plan_kernel, [c_tiles, square, to_tgt], swap(message, SRC), f_pot,
                              gain, scratch=row_scratch)
    for step_index in range(1, ITERS):
        if step_index > 1:
            (message,) = call(functools.partial(row_kernel, float(tgt_total)), [to_tgt],
                              swap(message, SRC), plan, scratch=row_scratch)
        (message,) = call(functools.partial(column_kernel, float(src_total)), [to_src],
                          swap(message, TGT), plan)
    tall = own_rows // 8 * (feats // LANES) * 8 + 8
    g_pot, part = call(
        functools.partial(final_kernel, float(tgt_total), own_rows),
        [c_tiles, (n_tgt, tall, LANES)], swap(message, SRC), lse, plan, columns,
        scratch=[pltpu.VMEM((feats + LANES, n_cols), jnp.bfloat16)] * 2)
    part = jnp.sum(swap(part.reshape(n_near, n_far * tall, LANES), NEAR), axis=0)
    part = swap(part.reshape(n_far, tall, LANES), FAR)
    (velocity,) = call(last_kernel, [noise.shape], part, noise)
    return velocity, g_pot.reshape(-1)


def solution(mesh):
    src, tgt = mesh.shape["src"], mesh.shape["tgt"]
    split = Mesh(mesh.devices.reshape(src // 2, 2, X_CHIPS, tgt // X_CHIPS // 2, 2), SRC + TGT)
    return jax.shard_map(
        per_device,
        mesh=split,
        in_specs=(P((*SRC, *TGT), None), P(TGT, SRC)),
        out_specs=(P((*SRC, *TGT), None), P(TGT)),
        check_vma=False,
    )
```

```python
import functools
import math

import jax
import jax.numpy as jnp
from jax import lax
from jax.experimental import pallas as pl
from jax.experimental.pallas import tpu as pltpu
from jax.sharding import Mesh, PartitionSpec as P

ITERS = 3


EPS = 0.05
LANES = 128
BLOCK = 256
X_CHIPS = 4
INTERPRET = False
LIMIT = 24 << 20
SRC, TGT, NEAR, FAR = ("y", "core"), ("x", "zh", "zb"), ("x", "zb"), "zh"
F32 = jnp.float32


def spread(value, axis):
    count = lax.axis_size(axis)
    return lax.all_to_all(jnp.broadcast_to(value[None], (count,) + value.shape), axis, 0, 0)


def diagonal():
    shape = (LANES, LANES)
    return lax.broadcasted_iota(jnp.int32, shape, 0) == lax.broadcasted_iota(jnp.int32, shape, 1)


def down(row):
    return jnp.sum(jnp.where(diagonal(), row, 0.0), axis=1, keepdims=True)


def across(column):
    return jnp.sum(jnp.where(diagonal(), column, 0.0), axis=0, keepdims=True)


def flat(tiles):
    return jnp.concatenate([tiles[t : t + 1] for t in range(tiles.shape[0])], axis=1)


def merged(ref):
    parts = ref[...]
    top = jnp.max(parts, axis=0)
    return top + jnp.log(jnp.sum(jnp.exp(parts - top[None]), axis=0))


def send(out_ref, tiles):
    out_ref[...] = jnp.broadcast_to(tiles[None], out_ref.shape)


def thirds(value):
    high = value.astype(jnp.bfloat16)
    rest = value - high.astype(F32)
    middle = rest.astype(jnp.bfloat16)
    return high, middle, (rest - middle.astype(F32)).astype(jnp.bfloat16)


LEFT, RIGHT = (2, 0, 1, 1, 0, 0), (0, 2, 1, 0, 1, 0)


def pile_kernel(*refs):
    for k, ref in enumerate(refs[:-1]):
        refs[-1][k] = ref[...]


def turned(hop, core, count):
    return hop * (1 - 2 * core) if abs(hop) < count // 2 else hop


def order_kernel(hops, count, mine_ref, theirs_ref, data_ref):
    at, core = lax.axis_index("y"), lax.axis_index("core")
    groups, halfs, deep, _ = mine_ref.shape
    for c, ref in enumerate((mine_ref, theirs_ref)):
        for k in range(groups):
            for h in range(halfs):
                owner = 1 - core if c else core
                back = turned(hops[k], owner, count) + h * (count // 2)
                spot = (2 * lax.rem(at + 2 * count - back, count) + owner) * deep
                data_ref[pl.ds(pl.multiple_of(spot, 8), deep), :] = ref[k, h]


def cost_kernel(data_ref, noise_ref, gain_ref, out_ref, rows_ref, terms_ref):
    data = data_ref[...]
    feats = data.shape[0]
    scale = 1.0 / (feats * EPS)
    data_sq = jnp.sum(data * data, axis=0, keepdims=True)
    parts = thirds(data)
    for k, which in enumerate(RIGHT):
        terms_ref[k * feats : (k + 1) * feats, :] = parts[which]
    for b in range(noise_ref.shape[0] // BLOCK):
        at = slice(b * BLOCK, (b + 1) * BLOCK)
        rows = noise_ref[at, :]
        parts = thirds(rows)
        cross = jnp.dot(jnp.concatenate([parts[which] for which in LEFT], axis=1),
                        terms_ref[...], preferred_element_type=F32)
        gain = (2.0 * cross - jnp.sum(rows * rows, axis=1, keepdims=True) - data_sq) * scale
        gain_ref[at, :] = gain
        top = jnp.max(gain, axis=1, keepdims=True)
        lse = top + jnp.log(jnp.sum(jnp.exp(gain - top), axis=1, keepdims=True))
        for t in range(BLOCK // LANES):
            spot = b * (BLOCK // LANES) + t
            rows_ref[spot : spot + 1, :] = across(lse[t * LANES : (t + 1) * LANES])
    send(out_ref, rows_ref[...])


def first_column_kernel(log_src, in_ref, gain_ref, f_ref, out_ref):
    f_pot = -(log_src + merged(in_ref))
    f_ref[...] = f_pot
    top = total = None
    for b in range(f_pot.shape[0]):
        z = gain_ref[b * LANES : (b + 1) * LANES, :] + down(f_pot[b : b + 1])
        here = jnp.max(z, axis=0, keepdims=True)
        if b == 0:
            top, total = here, jnp.sum(jnp.exp(z - here), axis=0, keepdims=True)
        else:
            new = jnp.maximum(top, here)
            total = total * jnp.exp(top - new) + jnp.sum(jnp.exp(z - new), axis=0, keepdims=True)
            top = new
    lse = top + jnp.log(total)
    for t in range(out_ref.shape[1]):
        out_ref[:, t : t + 1, :] = jnp.broadcast_to(
            lse[None, :, t * LANES : (t + 1) * LANES], (out_ref.shape[0], 1, LANES))


def plan_kernel(in_ref, f_ref, gain_ref, lse_ref, plan_ref, out_ref, rows_ref):
    lse = merged(in_ref)
    lse_ref[...] = lse
    column = flat(lse)
    for b in range(rows_ref.shape[0]):
        at = slice(b * LANES, (b + 1) * LANES)
        plan = jnp.exp((gain_ref[at, :] + down(f_ref[b : b + 1, :])) - column)
        plan_ref[at, :] = plan
        rows_ref[b : b + 1, :] = across(jnp.sum(plan, axis=1, keepdims=True))
    send(out_ref, rows_ref[...])


def column_kernel(src_total, in_ref, plan_ref, out_ref):
    u = 1.0 / (src_total * jnp.sum(in_ref[...], axis=0))
    total = jnp.zeros((1, plan_ref.shape[1]), F32)
    for b in range(u.shape[0]):
        total += jnp.sum(plan_ref[b * LANES : (b + 1) * LANES, :] * down(u[b : b + 1]),
                         axis=0, keepdims=True)
    for t in range(out_ref.shape[1]):
        out_ref[:, t : t + 1, :] = jnp.broadcast_to(
            total[None, :, t * LANES : (t + 1) * LANES], (out_ref.shape[0], 1, LANES))


def row_kernel(tgt_total, in_ref, plan_ref, out_ref, rows_ref):
    v = flat(1.0 / (tgt_total * jnp.sum(in_ref[...], axis=0)))
    for b in range(rows_ref.shape[0]):
        rows_ref[b : b + 1, :] = across(
            jnp.sum(plan_ref[b * LANES : (b + 1) * LANES, :] * v, axis=1, keepdims=True))
    send(out_ref, rows_ref[...])


def halves(value):
    high = value.astype(jnp.bfloat16)
    return high, (value - high.astype(F32)).astype(jnp.bfloat16)


def final_kernel(tgt_total, own_rows, in_ref, lse_ref, plan_ref, data_ref, g_ref, part_ref,
                 high_ref, low_ref):
    v = 1.0 / (tgt_total * jnp.sum(in_ref[...], axis=0))
    g_ref[...] = EPS * (jnp.log(v) - (math.log(tgt_total) + lse_ref[...]))
    v = flat(v)
    feats = data_ref.shape[0]
    scaled = data_ref[...] * v
    high_ref[:feats, :], low_ref[:feats, :] = halves(scaled)
    high_ref[feats:, :], low_ref[feats:, :] = halves(jnp.broadcast_to(v, (LANES, v.shape[1])))
    lane = lax.broadcasted_iota(jnp.int32, (8, LANES), 1)
    tiles, wide = own_rows // 8, feats // LANES

    def times(a, w_ref):
        return lax.dot_general(a, w_ref[...], (((1,), (1,)), ((), ())),
                               preferred_element_type=F32)

    for b in range(plan_ref.shape[0] // BLOCK):
        high, low = halves(plan_ref[b * BLOCK : (b + 1) * BLOCK, :])
        got = times(high, low_ref) + times(low, high_ref) + times(high, high_ref)
        for p in range(BLOCK // own_rows):
            peer = b * (BLOCK // own_rows) + p
            mass = jnp.zeros((8, LANES), F32)
            for r in range(tiles):
                at = slice(p * own_rows + r * 8, p * own_rows + r * 8 + 8)
                for c in range(wide):
                    part_ref[peer, (r * wide + c) * 8 : (r * wide + c + 1) * 8, :] = got[
                        at, c * LANES : (c + 1) * LANES]
                mass = jnp.where(lane // (LANES // tiles) == r, got[at, feats:], mass)
            part_ref[peer, tiles * wide * 8 :, :] = mass


def last_kernel(in_ref, noise_ref, out_ref):
    rows, feats = noise_ref.shape
    tiles, wide = rows // 8, feats // LANES
    parts = jnp.sum(in_ref[...], axis=0)
    mass = parts[tiles * wide * 8 :]
    for r in range(tiles):
        inverse = 1.0 / mass[:, r * (LANES // tiles) : r * (LANES // tiles) + 1]
        for c in range(wide):
            at = (r * wide + c) * 8
            spot = (slice(r * 8, r * 8 + 8), slice(c * LANES, (c + 1) * LANES))
            out_ref[spot] = parts[at : at + 8] * inverse - noise_ref[spot]


def call(kernel, outs, *args, scratch=(), limit=LIMIT):
    return pl.pallas_call(
        kernel,
        out_shape=[jax.ShapeDtypeStruct(o, F32) if isinstance(o, tuple) else o for o in outs],
        in_specs=[pl.BlockSpec(memory_space=pltpu.VMEM)] * len(args),
        out_specs=[pl.BlockSpec(memory_space=pltpu.VMEM)] * len(outs),
        scratch_shapes=list(scratch),
        compiler_params=pltpu.CompilerParams(vmem_limit_bytes=limit),
        interpret=INTERPRET,
    )(*args)


def gathered(noise, data):
    count = lax.axis_size("y")

    def shifted(value, hop):
        return lax.ppermute(value, SRC, [
            (2 * i + c, 2 * ((i + turned(hop, c, count)) % count) + c)
            for i in range(count) for c in range(2)])

    hops = [0] + [h for k in range(1, count // 4 + 1) for h in (k, -k)][: count // 2 - 1]
    own = data.T
    rows = spread(noise, FAR).reshape(-1, noise.shape[1])
    far = shifted(own, count // 2)
    both = jnp.stack([own, far])
    near = [shifted(both, h) for h in hops[1:]]
    rows = spread(rows, NEAR).reshape(-1, noise.shape[1])
    (mine,) = call(pile_kernel, [(count // 2, *both.shape)], both, *near, limit=8 << 20)
    theirs = lax.ppermute(mine, "core", [(0, 1), (1, 0)])
    (columns,) = call(functools.partial(order_kernel, hops, count),
                      [(2 * count * own.shape[0], own.shape[1])], mine, theirs,
                      limit=8 << 20)
    return rows, columns


def per_device(noise, data):
    own_rows, feats = noise.shape
    rows, columns = gathered(noise, data)
    n_rows, n_cols = rows.shape[0], columns.shape[1]
    n_src, n_tgt, n_near, n_far = (lax.axis_size(a) for a in (SRC, TGT, NEAR, FAR))
    src_total, tgt_total = n_rows * n_src, n_cols * n_tgt
    r_tiles, c_tiles = (n_rows // LANES, LANES), (n_cols // LANES, LANES)
    to_tgt, to_src = (n_tgt, *r_tiles), (n_src, *c_tiles)
    row_scratch = [pltpu.VMEM(r_tiles, F32)]
    square = (n_rows, n_cols)

    def swap(value, axis):
        return lax.all_to_all(value, axis, 0, 0)

    gain, message = call(
        cost_kernel, [square, to_tgt], columns, rows,
        scratch=row_scratch + [pltpu.VMEM((len(LEFT) * feats, n_cols), jnp.bfloat16)])
    f_pot, message = call(functools.partial(first_column_kernel, math.log(src_total)),
                          [r_tiles, to_src], swap(message, TGT), gain)
    lse, plan, message = call(plan_kernel, [c_tiles, square, to_tgt], swap(message, SRC), f_pot,
                              gain, scratch=row_scratch)
    for step_index in range(1, ITERS):
        if step_index > 1:
            (message,) = call(functools.partial(row_kernel, float(tgt_total)), [to_tgt],
                              swap(message, SRC), plan, scratch=row_scratch)
        (message,) = call(functools.partial(column_kernel, float(src_total)), [to_src],
                          swap(message, TGT), plan)
    tall = own_rows // 8 * (feats // LANES) * 8 + 8
    g_pot, part = call(
        functools.partial(final_kernel, float(tgt_total), own_rows),
        [c_tiles, (n_tgt, tall, LANES)], swap(message, SRC), lse, plan, columns,
        scratch=[pltpu.VMEM((feats + LANES, n_cols), jnp.bfloat16)] * 2)
    part = jnp.sum(swap(part.reshape(n_near, n_far * tall, LANES), NEAR), axis=0)
    part = swap(part.reshape(n_far, tall, LANES), FAR)
    (velocity,) = call(last_kernel, [noise.shape], part, noise)
    return velocity, g_pot.reshape(-1)


def solution(mesh):
    src, tgt = mesh.shape["src"], mesh.shape["tgt"]
    split = Mesh(mesh.devices.reshape(src // 2, 2, X_CHIPS, tgt // X_CHIPS // 2, 2), SRC + TGT)
    return jax.shard_map(
        per_device,
        mesh=split,
        in_specs=(P((*SRC, *TGT), None), P(TGT, SRC)),
        out_specs=(P((*SRC, *TGT), None), P(TGT)),
        check_vma=False,
    )
```

```python
import functools
import math

import jax
import jax.numpy as jnp
from jax import lax
from jax.experimental import pallas as pl
from jax.experimental.pallas import tpu as pltpu
from jax.sharding import Mesh, PartitionSpec as P

ITERS = 3


EPS = 0.05
LANES = 128
BLOCK = 256
X_CHIPS = 4
INTERPRET = False
LIMIT = 24 << 20
SRC, TGT, NEAR, FAR = ("y", "core"), ("x", "zh", "zb"), ("x", "zb"), "zh"
F32 = jnp.float32


def spread(value, axis):
    count = lax.axis_size(axis)
    return lax.all_to_all(jnp.broadcast_to(value[None], (count,) + value.shape), axis, 0, 0)


def diagonal():
    shape = (LANES, LANES)
    return lax.broadcasted_iota(jnp.int32, shape, 0) == lax.broadcasted_iota(jnp.int32, shape, 1)


def down(row):
    return jnp.sum(jnp.where(diagonal(), row, 0.0), axis=1, keepdims=True)


def across(column):
    return jnp.sum(jnp.where(diagonal(), column, 0.0), axis=0, keepdims=True)


def flat(tiles):
    return jnp.concatenate([tiles[t : t + 1] for t in range(tiles.shape[0])], axis=1)


def merged(ref):
    parts = ref[...]
    top = jnp.max(parts, axis=0)
    return top + jnp.log(jnp.sum(jnp.exp(parts - top[None]), axis=0))


def send(out_ref, tiles):
    out_ref[...] = jnp.broadcast_to(tiles[None], out_ref.shape)


def thirds(value):
    high = value.astype(jnp.bfloat16)
    rest = value - high.astype(F32)
    middle = rest.astype(jnp.bfloat16)
    return high, middle, (rest - middle.astype(F32)).astype(jnp.bfloat16)


LEFT, RIGHT = (2, 0, 1, 1, 0, 0), (0, 2, 1, 0, 1, 0)


def pile_kernel(*refs):
    for k, ref in enumerate(refs[:-1]):
        refs[-1][k] = ref[...]


def turned(hop, core, count):
    return hop * (1 - 2 * core) if abs(hop) < count // 2 else hop


def order_kernel(hops, count, mine_ref, theirs_ref, data_ref):
    at, core = lax.axis_index("y"), lax.axis_index("core")
    groups, halfs, deep, _ = mine_ref.shape
    for c, ref in enumerate((mine_ref, theirs_ref)):
        for k in range(groups):
            for h in range(halfs):
                owner = 1 - core if c else core
                back = turned(hops[k], owner, count) + h * (count // 2)
                spot = (2 * lax.rem(at + 2 * count - back, count) + owner) * deep
                data_ref[pl.ds(pl.multiple_of(spot, 8), deep), :] = ref[k, h]


def cost_kernel(data_ref, noise_ref, gain_ref, out_ref, rows_ref, terms_ref):
    data = data_ref[...]
    feats = data.shape[0]
    scale = 1.0 / (feats * EPS)
    data_sq = jnp.sum(data * data, axis=0, keepdims=True)
    parts = thirds(data)
    for k, which in enumerate(RIGHT):
        terms_ref[k * feats : (k + 1) * feats, :] = parts[which]
    for b in range(noise_ref.shape[0] // BLOCK):
        at = slice(b * BLOCK, (b + 1) * BLOCK)
        rows = noise_ref[at, :]
        parts = thirds(rows)
        cross = jnp.dot(jnp.concatenate([parts[which] for which in LEFT], axis=1),
                        terms_ref[...], preferred_element_type=F32)
        gain = (2.0 * cross - jnp.sum(rows * rows, axis=1, keepdims=True) - data_sq) * scale
        gain_ref[at, :] = gain
        top = jnp.max(gain, axis=1, keepdims=True)
        lse = top + jnp.log(jnp.sum(jnp.exp(gain - top), axis=1, keepdims=True))
        for t in range(BLOCK // LANES):
            spot = b * (BLOCK // LANES) + t
            rows_ref[spot : spot + 1, :] = across(lse[t * LANES : (t + 1) * LANES])
    send(out_ref, rows_ref[...])


def first_column_kernel(log_src, in_ref, gain_ref, f_ref, out_ref):
    f_pot = -(log_src + merged(in_ref))
    f_ref[...] = f_pot
    top = total = None
    for b in range(f_pot.shape[0]):
        z = gain_ref[b * LANES : (b + 1) * LANES, :] + down(f_pot[b : b + 1])
        here = jnp.max(z, axis=0, keepdims=True)
        if b == 0:
            top, total = here, jnp.sum(jnp.exp(z - here), axis=0, keepdims=True)
        else:
            new = jnp.maximum(top, here)
            total = total * jnp.exp(top - new) + jnp.sum(jnp.exp(z - new), axis=0, keepdims=True)
            top = new
    lse = top + jnp.log(total)
    for t in range(out_ref.shape[1]):
        out_ref[:, t : t + 1, :] = jnp.broadcast_to(
            lse[None, :, t * LANES : (t + 1) * LANES], (out_ref.shape[0], 1, LANES))


def plan_kernel(in_ref, f_ref, gain_ref, lse_ref, plan_ref, out_ref, rows_ref):
    lse = merged(in_ref)
    lse_ref[...] = lse
    column = flat(lse)
    for b in range(rows_ref.shape[0]):
        at = slice(b * LANES, (b + 1) * LANES)
        plan = jnp.exp((gain_ref[at, :] + down(f_ref[b : b + 1, :])) - column)
        plan_ref[at, :] = plan
        rows_ref[b : b + 1, :] = across(jnp.sum(plan, axis=1, keepdims=True))
    send(out_ref, rows_ref[...])


def column_kernel(src_total, in_ref, plan_ref, out_ref):
    u = 1.0 / (src_total * jnp.sum(in_ref[...], axis=0))
    total = jnp.zeros((1, plan_ref.shape[1]), F32)
    for b in range(u.shape[0]):
        total += jnp.sum(plan_ref[b * LANES : (b + 1) * LANES, :] * down(u[b : b + 1]),
                         axis=0, keepdims=True)
    for t in range(out_ref.shape[1]):
        out_ref[:, t : t + 1, :] = jnp.broadcast_to(
            total[None, :, t * LANES : (t + 1) * LANES], (out_ref.shape[0], 1, LANES))


def row_kernel(tgt_total, in_ref, plan_ref, out_ref, rows_ref):
    v = flat(1.0 / (tgt_total * jnp.sum(in_ref[...], axis=0)))
    for b in range(rows_ref.shape[0]):
        rows_ref[b : b + 1, :] = across(
            jnp.sum(plan_ref[b * LANES : (b + 1) * LANES, :] * v, axis=1, keepdims=True))
    send(out_ref, rows_ref[...])


def halves(value):
    high = value.astype(jnp.bfloat16)
    return high, (value - high.astype(F32)).astype(jnp.bfloat16)


def final_kernel(tgt_total, own_rows, n_far, in_ref, lse_ref, plan_ref, data_ref, g_ref, part_ref,
                 high_ref, low_ref):
    v = 1.0 / (tgt_total * jnp.sum(in_ref[...], axis=0))
    g_ref[...] = EPS * (jnp.log(v) - (math.log(tgt_total) + lse_ref[...]))
    v = flat(v)
    feats = data_ref.shape[0]
    scaled = data_ref[...] * v
    high_ref[:feats, :], low_ref[:feats, :] = halves(scaled)
    high_ref[feats:, :], low_ref[feats:, :] = halves(jnp.broadcast_to(v, (LANES, v.shape[1])))
    tiles, wide = own_rows // 8, feats // LANES
    tall = tiles * wide * 8
    own = [lax.broadcasted_iota(jnp.int32, (own_rows, LANES), d) for d in range(2)]

    def times(a, w_ref):
        return lax.dot_general(a, w_ref[...], (((1,), (1,)), ((), ())),
                               preferred_element_type=F32)

    part_ref[:, n_far * tall :, :] = jnp.zeros((part_ref.shape[0], 8, LANES), F32)
    for b in range(plan_ref.shape[0] // BLOCK):
        high, low = halves(plan_ref[b * BLOCK : (b + 1) * BLOCK, :])
        got = times(high, low_ref) + times(low, high_ref) + times(high, high_ref)
        for p in range(BLOCK // own_rows):
            near, far = divmod(b * (BLOCK // own_rows) + p, n_far)
            for r in range(tiles):
                at = slice(p * own_rows + r * 8, p * own_rows + r * 8 + 8)
                for c in range(wide):
                    spot = far * tall + (r * wide + c) * 8
                    part_ref[near, spot : spot + 8, :] = got[at, c * LANES : (c + 1) * LANES]
            mass = got[p * own_rows : (p + 1) * own_rows, feats:]
            part_ref[near, n_far * tall + far : n_far * tall + far + 1, :] = jnp.sum(
                jnp.where(own[0] == own[1], mass, 0.0), axis=0, keepdims=True)


def last_kernel(in_ref, noise_ref, out_ref):
    rows, feats = noise_ref.shape
    tiles, wide = rows // 8, feats // LANES
    parts = jnp.sum(in_ref[...], axis=0)
    masses = parts[tiles * wide * 8 :]
    mine = lax.broadcasted_iota(jnp.int32, masses.shape, 0) == lax.axis_index(FAR)
    inverse = 1.0 / down(jnp.sum(jnp.where(mine, masses, 0.0), axis=0, keepdims=True))[:rows]
    for r in range(tiles):
        for c in range(wide):
            at = (r * wide + c) * 8
            spot = (slice(r * 8, r * 8 + 8), slice(c * LANES, (c + 1) * LANES))
            out_ref[spot] = parts[at : at + 8] * inverse[spot[0]] - noise_ref[spot]


def call(kernel, outs, *args, scratch=(), limit=LIMIT):
    return pl.pallas_call(
        kernel,
        out_shape=[jax.ShapeDtypeStruct(o, F32) if isinstance(o, tuple) else o for o in outs],
        in_specs=[pl.BlockSpec(memory_space=pltpu.VMEM)] * len(args),
        out_specs=[pl.BlockSpec(memory_space=pltpu.VMEM)] * len(outs),
        scratch_shapes=list(scratch),
        compiler_params=pltpu.CompilerParams(vmem_limit_bytes=limit),
        interpret=INTERPRET,
    )(*args)


def gathered(noise, data):
    count = lax.axis_size("y")

    def shifted(value, hop):
        return lax.ppermute(value, SRC, [
            (2 * i + c, 2 * ((i + turned(hop, c, count)) % count) + c)
            for i in range(count) for c in range(2)])

    hops = [0] + [h for k in range(1, count // 4 + 1) for h in (k, -k)][: count // 2 - 1]
    own = data.T
    rows = spread(noise, FAR).reshape(-1, noise.shape[1])
    far = shifted(own, count // 2)
    both = jnp.stack([own, far])
    near = [shifted(both, h) for h in hops[1:]]
    rows = spread(rows, NEAR).reshape(-1, noise.shape[1])
    (mine,) = call(pile_kernel, [(count // 2, *both.shape)], both, *near, limit=8 << 20)
    theirs = lax.ppermute(mine, "core", [(0, 1), (1, 0)])
    (columns,) = call(functools.partial(order_kernel, hops, count),
                      [(2 * count * own.shape[0], own.shape[1])], mine, theirs,
                      limit=8 << 20)
    return rows, columns


def per_device(noise, data):
    own_rows, feats = noise.shape
    rows, columns = gathered(noise, data)
    n_rows, n_cols = rows.shape[0], columns.shape[1]
    n_src, n_tgt, n_near, n_far = (lax.axis_size(a) for a in (SRC, TGT, NEAR, FAR))
    src_total, tgt_total = n_rows * n_src, n_cols * n_tgt
    r_tiles, c_tiles = (n_rows // LANES, LANES), (n_cols // LANES, LANES)
    to_tgt, to_src = (n_tgt, *r_tiles), (n_src, *c_tiles)
    row_scratch = [pltpu.VMEM(r_tiles, F32)]
    square = (n_rows, n_cols)

    def swap(value, axis):
        return lax.all_to_all(value, axis, 0, 0)

    gain, message = call(
        cost_kernel, [square, to_tgt], columns, rows,
        scratch=row_scratch + [pltpu.VMEM((len(LEFT) * feats, n_cols), jnp.bfloat16)])
    f_pot, message = call(functools.partial(first_column_kernel, math.log(src_total)),
                          [r_tiles, to_src], swap(message, TGT), gain)
    lse, plan, message = call(plan_kernel, [c_tiles, square, to_tgt], swap(message, SRC), f_pot,
                              gain, scratch=row_scratch)
    for step_index in range(1, ITERS):
        if step_index > 1:
            (message,) = call(functools.partial(row_kernel, float(tgt_total)), [to_tgt],
                              swap(message, SRC), plan, scratch=row_scratch)
        (message,) = call(functools.partial(column_kernel, float(src_total)), [to_src],
                          swap(message, TGT), plan)
    tall = own_rows // 8 * (feats // LANES) * 8
    g_pot, part = call(
        functools.partial(final_kernel, float(tgt_total), own_rows, n_far),
        [c_tiles, (n_near, n_far * tall + 8, LANES)], swap(message, SRC), lse, plan, columns,
        scratch=[pltpu.VMEM((feats + LANES, n_cols), jnp.bfloat16)] * 2)
    part = jnp.sum(swap(part, NEAR), axis=0)
    masses = jnp.broadcast_to(part[None, n_far * tall :], (n_far, 8, LANES))
    part = jnp.concatenate([part[: n_far * tall].reshape(n_far, tall, LANES), masses], axis=1)
    part = swap(part, FAR)
    (velocity,) = call(last_kernel, [noise.shape], part, noise)
    return velocity, g_pot.reshape(-1)


def solution(mesh):
    src, tgt = mesh.shape["src"], mesh.shape["tgt"]
    split = Mesh(mesh.devices.reshape(src // 2, 2, X_CHIPS, tgt // X_CHIPS // 2, 2), SRC + TGT)
    return jax.shard_map(
        per_device,
        mesh=split,
        in_specs=(P((*SRC, *TGT), None), P(TGT, SRC)),
        out_specs=(P((*SRC, *TGT), None), P(TGT)),
        check_vma=False,
    )
```

```python
import functools
import math

import jax
import jax.numpy as jnp
from jax import lax
from jax.experimental import pallas as pl
from jax.experimental.pallas import tpu as pltpu
from jax.sharding import Mesh, PartitionSpec as P

ITERS = 3


EPS = 0.05
LANES = 128
BLOCK = 256
X_CHIPS = 4
INTERPRET = False
LIMIT = 24 << 20
SRC, TGT, NEAR, FAR = ("y", "core"), ("x", "zh", "zb"), ("zb", "x"), "zh"
F32 = jnp.float32


def spread(value, axis):
    count = lax.axis_size(axis)
    return lax.all_to_all(jnp.broadcast_to(value[None], (count,) + value.shape), axis, 0, 0)


def diagonal():
    shape = (LANES, LANES)
    return lax.broadcasted_iota(jnp.int32, shape, 0) == lax.broadcasted_iota(jnp.int32, shape, 1)


def down(row):
    return jnp.sum(jnp.where(diagonal(), row, 0.0), axis=1, keepdims=True)


def across(column):
    return jnp.sum(jnp.where(diagonal(), column, 0.0), axis=0, keepdims=True)


def flat(tiles):
    return jnp.concatenate([tiles[t : t + 1] for t in range(tiles.shape[0])], axis=1)


def merged(ref):
    parts = ref[...]
    top = jnp.max(parts, axis=0)
    return top + jnp.log(jnp.sum(jnp.exp(parts - top[None]), axis=0))


def send(out_ref, tiles):
    out_ref[...] = jnp.broadcast_to(tiles[None], out_ref.shape)


def thirds(value):
    high = value.astype(jnp.bfloat16)
    rest = value - high.astype(F32)
    middle = rest.astype(jnp.bfloat16)
    return high, middle, (rest - middle.astype(F32)).astype(jnp.bfloat16)


LEFT, RIGHT = (2, 0, 1, 1, 0, 0), (0, 2, 1, 0, 1, 0)


def pile_kernel(*refs):
    for k, ref in enumerate(refs[:-1]):
        refs[-1][k] = ref[...]


def turned(hop, core, count):
    return hop * (1 - 2 * core) if abs(hop) < count // 2 else hop


def order_kernel(hops, count, mine_ref, theirs_ref, data_ref):
    at, core = lax.axis_index("y"), lax.axis_index("core")
    groups, halfs, deep, _ = mine_ref.shape
    for c, ref in enumerate((mine_ref, theirs_ref)):
        for k in range(groups):
            for h in range(halfs):
                owner = 1 - core if c else core
                back = turned(hops[k], owner, count) + h * (count // 2)
                spot = (2 * lax.rem(at + 2 * count - back, count) + owner) * deep
                data_ref[pl.ds(pl.multiple_of(spot, 8), deep), :] = ref[k, h]


def cost_kernel(data_ref, noise_ref, gain_ref, out_ref, rows_ref, terms_ref):
    data = data_ref[...]
    feats = data.shape[0]
    scale = 1.0 / (feats * EPS)
    data_sq = jnp.sum(data * data, axis=0, keepdims=True)
    parts = thirds(data)
    for k, which in enumerate(RIGHT):
        terms_ref[k * feats : (k + 1) * feats, :] = parts[which]
    for b in range(noise_ref.shape[0] // BLOCK):
        at = slice(b * BLOCK, (b + 1) * BLOCK)
        rows = noise_ref[at, :]
        parts = thirds(rows)
        cross = jnp.dot(jnp.concatenate([parts[which] for which in LEFT], axis=1),
                        terms_ref[...], preferred_element_type=F32)
        gain = (2.0 * cross - jnp.sum(rows * rows, axis=1, keepdims=True) - data_sq) * scale
        gain_ref[at, :] = gain
        top = jnp.max(gain, axis=1, keepdims=True)
        lse = top + jnp.log(jnp.sum(jnp.exp(gain - top), axis=1, keepdims=True))
        for t in range(BLOCK // LANES):
            spot = b * (BLOCK // LANES) + t
            rows_ref[spot : spot + 1, :] = across(lse[t * LANES : (t + 1) * LANES])
    send(out_ref, rows_ref[...])


def first_column_kernel(log_src, in_ref, gain_ref, f_ref, out_ref):
    f_pot = -(log_src + merged(in_ref))
    f_ref[...] = f_pot
    blocks, wide = range(f_pot.shape[0]), gain_ref.shape[1]
    columns = [down(f_pot[b : b + 1]) for b in blocks]

    def tiles(b):
        z = gain_ref[b * LANES : (b + 1) * LANES, :] + columns[b]
        return z.reshape(LANES // 8, 8, wide)

    top = functools.reduce(jnp.maximum, [jnp.max(tiles(b), axis=0) for b in blocks])
    top = jnp.max(top, axis=0, keepdims=True)
    total = sum(jnp.sum(jnp.exp(tiles(b) - top[None]), axis=0) for b in blocks)
    total = jnp.sum(total, axis=0, keepdims=True)
    lse = top + jnp.log(total)
    for t in range(out_ref.shape[1]):
        out_ref[:, t : t + 1, :] = jnp.broadcast_to(
            lse[None, :, t * LANES : (t + 1) * LANES], (out_ref.shape[0], 1, LANES))


def plan_kernel(in_ref, f_ref, gain_ref, lse_ref, plan_ref, out_ref, rows_ref):
    lse = merged(in_ref)
    lse_ref[...] = lse
    column = flat(lse)
    for b in range(rows_ref.shape[0]):
        at = slice(b * LANES, (b + 1) * LANES)
        plan = jnp.exp((gain_ref[at, :] + down(f_ref[b : b + 1, :])) - column)
        plan_ref[at, :] = plan
        rows_ref[b : b + 1, :] = across(jnp.sum(plan, axis=1, keepdims=True))
    send(out_ref, rows_ref[...])


def column_kernel(src_total, in_ref, plan_ref, out_ref):
    u = 1.0 / (src_total * jnp.sum(in_ref[...], axis=0))
    total = jnp.zeros((1, plan_ref.shape[1]), F32)
    for b in range(u.shape[0]):
        total += jnp.sum(plan_ref[b * LANES : (b + 1) * LANES, :] * down(u[b : b + 1]),
                         axis=0, keepdims=True)
    for t in range(out_ref.shape[1]):
        out_ref[:, t : t + 1, :] = jnp.broadcast_to(
            total[None, :, t * LANES : (t + 1) * LANES], (out_ref.shape[0], 1, LANES))


def row_kernel(tgt_total, in_ref, plan_ref, out_ref, rows_ref):
    v = flat(1.0 / (tgt_total * jnp.sum(in_ref[...], axis=0)))
    for b in range(rows_ref.shape[0]):
        rows_ref[b : b + 1, :] = across(
            jnp.sum(plan_ref[b * LANES : (b + 1) * LANES, :] * v, axis=1, keepdims=True))
    send(out_ref, rows_ref[...])


def halves(value):
    high = value.astype(jnp.bfloat16)
    return high, (value - high.astype(F32)).astype(jnp.bfloat16)


def final_kernel(tgt_total, own_rows, n_far, in_ref, lse_ref, plan_ref, data_ref, g_ref, part_ref,
                 high_ref, low_ref):
    v = 1.0 / (tgt_total * jnp.sum(in_ref[...], axis=0))
    g_ref[...] = EPS * (jnp.log(v) - (math.log(tgt_total) + lse_ref[...]))
    v = flat(v)
    feats = data_ref.shape[0]
    scaled = data_ref[...] * v
    high_ref[:feats, :], low_ref[:feats, :] = halves(scaled)
    high_ref[feats:, :], low_ref[feats:, :] = halves(jnp.broadcast_to(v, (LANES, v.shape[1])))
    tiles, wide = own_rows // 8, feats // LANES
    tall = tiles * wide * 8
    own = [lax.broadcasted_iota(jnp.int32, (own_rows, LANES), d) for d in range(2)]

    def times(a, w_ref):
        return lax.dot_general(a, w_ref[...], (((1,), (1,)), ((), ())),
                               preferred_element_type=F32)

    part_ref[:, n_far * tall :, :] = jnp.zeros((part_ref.shape[0], 8, LANES), F32)
    for b in range(plan_ref.shape[0] // BLOCK):
        high, low = halves(plan_ref[b * BLOCK : (b + 1) * BLOCK, :])
        got = times(high, low_ref) + times(low, high_ref) + times(high, high_ref)
        for p in range(BLOCK // own_rows):
            near, far = divmod(b * (BLOCK // own_rows) + p, n_far)
            for r in range(tiles):
                at = slice(p * own_rows + r * 8, p * own_rows + r * 8 + 8)
                for c in range(wide):
                    spot = far * tall + (r * wide + c) * 8
                    part_ref[near, spot : spot + 8, :] = got[at, c * LANES : (c + 1) * LANES]
            mass = got[p * own_rows : (p + 1) * own_rows, feats:]
            part_ref[near, n_far * tall + far : n_far * tall + far + 1, :] = jnp.sum(
                jnp.where(own[0] == own[1], mass, 0.0), axis=0, keepdims=True)


def last_kernel(in_ref, noise_ref, out_ref):
    rows, feats = noise_ref.shape
    tiles, wide = rows // 8, feats // LANES
    parts = jnp.sum(in_ref[...], axis=0)
    masses = parts[tiles * wide * 8 :]
    mine = lax.broadcasted_iota(jnp.int32, masses.shape, 0) == lax.axis_index(FAR)
    inverse = 1.0 / down(jnp.sum(jnp.where(mine, masses, 0.0), axis=0, keepdims=True))[:rows]
    for r in range(tiles):
        for c in range(wide):
            at = (r * wide + c) * 8
            spot = (slice(r * 8, r * 8 + 8), slice(c * LANES, (c + 1) * LANES))
            out_ref[spot] = parts[at : at + 8] * inverse[spot[0]] - noise_ref[spot]


def call(kernel, outs, *args, scratch=(), limit=LIMIT):
    return pl.pallas_call(
        kernel,
        out_shape=[jax.ShapeDtypeStruct(o, F32) if isinstance(o, tuple) else o for o in outs],
        in_specs=[pl.BlockSpec(memory_space=pltpu.VMEM)] * len(args),
        out_specs=[pl.BlockSpec(memory_space=pltpu.VMEM)] * len(outs),
        scratch_shapes=list(scratch),
        compiler_params=pltpu.CompilerParams(vmem_limit_bytes=limit),
        interpret=INTERPRET,
    )(*args)


def gathered(noise, data):
    count = lax.axis_size("y")

    def shifted(value, hop):
        return lax.ppermute(value, SRC, [
            (2 * i + c, 2 * ((i + turned(hop, c, count)) % count) + c)
            for i in range(count) for c in range(2)])

    hops = [0] + [h for k in range(1, count // 4 + 1) for h in (k, -k)][: count // 2 - 1]
    own = data.T
    rows = spread(noise, FAR).reshape(-1, noise.shape[1])
    far = shifted(own, count // 2)
    both = jnp.stack([own, far])
    near = [shifted(both, h) for h in hops[1:]]
    rows = spread(rows, NEAR).reshape(-1, noise.shape[1])
    (mine,) = call(pile_kernel, [(count // 2, *both.shape)], both, *near, limit=8 << 20)
    theirs = lax.ppermute(mine, "core", [(0, 1), (1, 0)])
    (columns,) = call(functools.partial(order_kernel, hops, count),
                      [(2 * count * own.shape[0], own.shape[1])], mine, theirs,
                      limit=8 << 20)
    return rows, columns


def per_device(noise, data):
    own_rows, feats = noise.shape
    rows, columns = gathered(noise, data)
    n_rows, n_cols = rows.shape[0], columns.shape[1]
    n_src, n_tgt, n_near, n_far = (lax.axis_size(a) for a in (SRC, TGT, NEAR, FAR))
    src_total, tgt_total = n_rows * n_src, n_cols * n_tgt
    r_tiles, c_tiles = (n_rows // LANES, LANES), (n_cols // LANES, LANES)
    to_tgt, to_src = (n_tgt, *r_tiles), (n_src, *c_tiles)
    row_scratch = [pltpu.VMEM(r_tiles, F32)]
    square = (n_rows, n_cols)

    def swap(value, axis):
        return lax.all_to_all(value, axis, 0, 0)

    gain, message = call(
        cost_kernel, [square, to_tgt], columns, rows,
        scratch=row_scratch + [pltpu.VMEM((len(LEFT) * feats, n_cols), jnp.bfloat16)])
    f_pot, message = call(functools.partial(first_column_kernel, math.log(src_total)),
                          [r_tiles, to_src], swap(message, TGT), gain)
    lse, plan, message = call(plan_kernel, [c_tiles, square, to_tgt], swap(message, SRC), f_pot,
                              gain, scratch=row_scratch)
    for step_index in range(1, ITERS):
        if step_index > 1:
            (message,) = call(functools.partial(row_kernel, float(tgt_total)), [to_tgt],
                              swap(message, SRC), plan, scratch=row_scratch)
        (message,) = call(functools.partial(column_kernel, float(src_total)), [to_src],
                          swap(message, TGT), plan)
    tall = own_rows // 8 * (feats // LANES) * 8
    g_pot, part = call(
        functools.partial(final_kernel, float(tgt_total), own_rows, n_far),
        [c_tiles, (n_near, n_far * tall + 8, LANES)], swap(message, SRC), lse, plan, columns,
        scratch=[pltpu.VMEM((feats + LANES, n_cols), jnp.bfloat16)] * 2)
    part = jnp.sum(swap(part, NEAR), axis=0)
    masses = jnp.broadcast_to(part[None, n_far * tall :], (n_far, 8, LANES))
    part = jnp.concatenate([part[: n_far * tall].reshape(n_far, tall, LANES), masses], axis=1)
    part = swap(part, FAR)
    (velocity,) = call(last_kernel, [noise.shape], part, noise)
    return velocity, g_pot.reshape(-1)


def solution(mesh):
    src, tgt = mesh.shape["src"], mesh.shape["tgt"]
    split = Mesh(mesh.devices.reshape(src // 2, 2, X_CHIPS, tgt // X_CHIPS // 2, 2), SRC + TGT)
    return jax.shard_map(
        per_device,
        mesh=split,
        in_specs=(P((*SRC, *TGT), None), P(TGT, SRC)),
        out_specs=(P((*SRC, *TGT), None), P(TGT)),
        check_vma=False,
    )
```
